32 devices in a mesh: dp: 4 (over y, x), tm: 8 (over z, core).
Axes of the slice: x: 2, y: 2, z: 4, core: 2. Of those that a mesh axis runs over, the one named last changes fastest.
Arguments:
- frames: bfloat16 [16384, 1024], P(('dp', 'tm')), parts along dimension 0, may hold values from -6 to 6
- norm_gain1: float32 [1024], replicated, may hold values from 0.1 to 1.9
- w_qkv1: bfloat16 [1024, 1536], replicated, may hold values from -0.1875 to 0.1875
- log_decay: float32 [8, 16384], P(None, ('dp', 'tm')), parts along dimension 1, may hold values from -0.8 to 0, as said below
- head_gain: float32 [512], replicated, may hold values from 0.1 to 1.9
- w_out1: bfloat16 [512, 1024], replicated, may hold values from -0.25 to 0.25
- norm_gain2: float32 [1024], replicated, may hold values from 0.1 to 1.9
- w_qkv2: bfloat16 [1024, 1536], replicated, may hold values from -4 to 4
- window_ids: int32 [32, 2], P(('dp', 'tm')), parts along dimension 0, may hold values from -1 to 6, as said below
- w_out2: bfloat16 [512, 1024], replicated, may hold values from -0.25 to 0.25
Outputs:
- context: bfloat16 [16384, 1024], P(('dp', 'tm')), parts along dimension 0
The draws below stay inside these ranges and needn't reach their ends.
There are 4 independent parts, one for each index of `dp`. The reference program is written for one: setup_inputs(seed, part) draws one part's arguments, and reference() takes and returns one part's arrays. A program takes and returns all parts, laid end to end along the dimension named above; an argument that names none is the same for every part. Nothing has to cross between parts.
Inputs may be any that keep to these rules, and one draw needn't show every extreme that they name: `log_decay`: values are at most 0; in each head the decay varies over the frames. `window_ids`: row j holds distinct ids of blocks j - 3 to j - 1, or -1 for an empty slot; rows hold different numbers of ids, and some rows none. The last row lists 2 blocks, among them the blocks 1 and 3 before it.
All inputs are finite; a program needn't handle non-finite values.
Results may differ from the reference program's by a relative error of at most 0.0072.
Values may be sent and summed in bfloat16 or wider, within the bound.
A program may use at most 128 MiB of HBM per device.

```python
import math
import jax
import jax.numpy as jnp
from jax import lax

D = 1024
HALF_HEAD_COUNT = 8
HD = 64
BLK = 512
GROUP = 256
LIST = 2
REACH_BLOCKS = 3
UTTERANCE_FRAMES = 4096
NB = 8


def draw_log_decay(key, part):
    parallel_sequences = jax.random.split(key, 6)
    slow = jax.random.randint(parallel_sequences[0], (HALF_HEAD_COUNT, 1), 0, 10) < 5
    slow_rate = jax.random.uniform(parallel_sequences[1], (HALF_HEAD_COUNT, 1), jnp.float32, 0.2, 0.8) / UTTERANCE_FRAMES
    fast_rate = 1.0 / jax.random.uniform(parallel_sequences[2], (HALF_HEAD_COUNT, 1), jnp.float32, 30.0, 50.0)
    baseline_decay_rate = jnp.where(slow, slow_rate, fast_rate)
    coarse_estimate = jnp.exp(jax.random.uniform(parallel_sequences[3], (HALF_HEAD_COUNT, UTTERANCE_FRAMES), jnp.float32, math.log(0.5), math.log(2.0)))
    spike_position = jax.random.randint(parallel_sequences[4], (1, UTTERANCE_FRAMES), 0, UTTERANCE_FRAMES) < 3
    spike_magnitude = jnp.where(spike_position, jnp.log(jax.random.uniform(parallel_sequences[5], (HALF_HEAD_COUNT, UTTERANCE_FRAMES), jnp.float32, 0.5, 0.8)), 0.0)
    return (-baseline_decay_rate * coarse_estimate + spike_magnitude).astype(jnp.float32)


def draw_w_qkv2(key, part):
    parallel_sequences = jax.random.split(key, 1)
    width = HALF_HEAD_COUNT * HD
    weights = jnp.clip(jax.random.normal(parallel_sequences[0], (D, 3 * width), jnp.float32), -6.0, 6.0) * D ** (-0.5)
    return weights.astype(jnp.bfloat16)


def draw_window_ids(key, part):
    parallel_sequences = jax.random.split(key, 3)
    rows = jnp.arange(NB, dtype=jnp.int32)[:, None]
    offsets = jnp.arange(1, REACH_BLOCKS + 1, dtype=jnp.int32)[None, :]
    scores = jax.random.randint(parallel_sequences[0], (NB, REACH_BLOCKS), 0, 100000) * (2 * REACH_BLOCKS) + offsets
    last = rows == NB - 1
    far = (jax.random.randint(parallel_sequences[1], (NB, 1), 0, 2) == 1) | last
    scores = scores + jnp.where(far & (offsets == REACH_BLOCKS), 10000000, 0)
    scores = scores + jnp.where(last & (offsets == 1), 5000000, 0)
    order = jnp.argsort(-scores, axis=1, stable=True)[:, :LIST].astype(jnp.int32)
    chosen = order + 1
    counts = jax.random.randint(parallel_sequences[2], (NB, 1), 1, LIST + 1)
    counts = jnp.where(last, LIST, counts)
    slots = jnp.arange(LIST, dtype=jnp.int32)[None, :]
    ids = rows - chosen
    valid = (slots < counts) & (ids >= 0)
    return jnp.where(valid, ids, -1).astype(jnp.int32)


def level_of(stream_key, dims, cuts, smallest, top_value):
    level, own = 1.0, jax.random.fold_in(stream_key, 6)
    for axis_at, blocks in cuts:
        steps = jnp.exp(jax.random.uniform(jax.random.fold_in(own, axis_at), (blocks,), jnp.float32, smallest / len(cuts), top_value / len(cuts)))
        level = level * jnp.repeat(steps, dims[axis_at] // blocks).reshape([-1 if axis == axis_at else 1 for axis in range(len(dims))])
    return level


def centred(own_key, extent, scale, limit, cuts=(), kind=jnp.bfloat16):
    drawn = jax.random.normal(own_key, extent, jnp.float32) * scale
    if len(cuts) > 0:
        drawn = level_of(own_key, extent, cuts, -0.22, 0.18) * drawn
    return jnp.clip(drawn, min=-limit, max=limit).astype(kind)


def setup_inputs(seed: int = 0, part: int = 0) -> dict:
    key_list = jax.random.split(jax.random.key(seed), 11)
    part_splits = jax.random.split(jax.random.fold_in(key_list[10], part), 11)
    frames = centred(part_splits[0], (UTTERANCE_FRAMES, D), 1.0, 6.0, ((0, 8),))
    norm_gain1 = jnp.clip(1.0 + 0.18 * jax.random.normal(key_list[1], (D,), jnp.float32), 0.1, 1.9)
    w_qkv1 = centred(key_list[2], (D, 3 * HALF_HEAD_COUNT * HD), D ** -0.5, 0.1875)
    log_decay = draw_log_decay(jax.random.fold_in(jax.random.fold_in(key_list[10], part), 71), part)
    head_gain = jnp.clip(1.0 + 0.18 * jax.random.normal(key_list[4], (HALF_HEAD_COUNT * HD,), jnp.float32), 0.1, 1.9)
    w_out1 = centred(key_list[5], (HALF_HEAD_COUNT * HD, D), (HALF_HEAD_COUNT * HD) ** -0.5, 0.25)
    norm_gain2 = jnp.clip(1.0 + 0.18 * jax.random.normal(key_list[6], (D,), jnp.float32), 0.1, 1.9)
    w_qkv2 = draw_w_qkv2(jax.random.fold_in(key_list[10], 71), part)
    window_ids = draw_window_ids(jax.random.fold_in(jax.random.fold_in(key_list[10], part), 71), part)
    w_out2 = centred(key_list[9], (HALF_HEAD_COUNT * HD, D), (HALF_HEAD_COUNT * HD) ** -0.5, 0.25)
    return {"frames": frames, "norm_gain1": norm_gain1, "w_qkv1": w_qkv1, "log_decay": log_decay, "head_gain": head_gain, "w_out1": w_out1, "norm_gain2": norm_gain2, "w_qkv2": w_qkv2, "window_ids": window_ids, "w_out2": w_out2}


def rms_norm(values, gain):
    wide = values.astype(jnp.float32)
    scale = lax.rsqrt(lax.optimization_barrier(jnp.mean(wide * wide, axis=-1, keepdims=True)) + 1e-05)
    return (wide * scale * gain).astype(jnp.bfloat16)

def group_step(state, inputs):
    query, key_part, value, decay = inputs
    cumul = jnp.cumsum(decay, axis=0)
    scores = jnp.einsum('thd,shd->hts', query.astype(jnp.float32), key_part.astype(jnp.float32))
    trans = cumul.T
    diff = trans[:, :, None] - trans[:, None, :]
    length = decay.shape[0]
    causal = jnp.arange(length)[:, None] >= jnp.arange(length)[None, :]
    weight = jnp.where(causal[None], jnp.exp(jnp.minimum(diff, 0.0)), 0.0)
    mix = (scores * weight).astype(jnp.bfloat16)
    intra = jnp.einsum('hts,shd->thd', mix.astype(jnp.float32), value.astype(jnp.float32))
    scaled = query.astype(jnp.float32) * jnp.exp(cumul)[:, :, None]
    inter = jnp.einsum('thd,hde->the', scaled, state, precision=lax.Precision.HIGHEST)
    keyed = key_part.astype(jnp.float32) * jnp.exp(cumul[-1][None, :] - cumul)[:, :, None]
    update = jnp.einsum('shd,she->hde', keyed, value.astype(jnp.float32), precision=lax.Precision.HIGHEST)
    state = jnp.exp(cumul[-1])[:, None, None] * state + update
    return (state, intra + inter)

def reference(frames, norm_gain1, w_qkv1, log_decay, head_gain, w_out1, norm_gain2, w_qkv2, window_ids, w_out2):
    width = HALF_HEAD_COUNT * HD
    h_one = rms_norm(frames, norm_gain1)
    qkv = jnp.dot(h_one, w_qkv1, preferred_element_type=jnp.float32).astype(jnp.bfloat16)
    count = UTTERANCE_FRAMES // GROUP
    query = qkv[:, :width].reshape(count, GROUP, HALF_HEAD_COUNT, HD)
    key_part = qkv[:, width:2 * width].reshape(count, GROUP, HALF_HEAD_COUNT, HD)
    value = qkv[:, 2 * width:].reshape(count, GROUP, HALF_HEAD_COUNT, HD)
    decay = log_decay.T.reshape(count, GROUP, HALF_HEAD_COUNT)
    start = jnp.zeros((HALF_HEAD_COUNT, HD, HD), jnp.float32)
    final, lin = lax.scan(group_step, start, (query, key_part, value, decay))
    lin = lin.reshape(UTTERANCE_FRAMES, HALF_HEAD_COUNT, HD)
    normed = lin * lax.rsqrt(lax.optimization_barrier(jnp.mean(lin * lin, axis=-1, keepdims=True)) + 1e-06)
    y_one = (normed.reshape(UTTERANCE_FRAMES, width) * head_gain).astype(jnp.bfloat16)
    branch = jnp.dot(y_one, w_out1, preferred_element_type=jnp.float32)
    hidden1 = (frames.astype(jnp.float32) + branch).astype(jnp.bfloat16)
    h_two = rms_norm(hidden1, norm_gain2)
    qkv2 = jnp.dot(h_two, w_qkv2, preferred_element_type=jnp.float32).astype(jnp.bfloat16)
    q_blocks = qkv2[:, :width].reshape(NB, BLK, HALF_HEAD_COUNT, HD)
    k_blocks = qkv2[:, width:2 * width].reshape(NB, BLK, HALF_HEAD_COUNT, HD)
    v_blocks = qkv2[:, 2 * width:].reshape(NB, BLK, HALF_HEAD_COUNT, HD)
    causal = jnp.arange(BLK)[:, None] >= jnp.arange(BLK)[None, :]

    def one_block(index):
        ids = window_ids[index]
        valid = ids >= 0
        safe = jnp.clip(ids, 0, NB - 1).astype(jnp.int32)
        key_lines = jnp.concatenate([k_blocks[safe].reshape(LIST * BLK, HALF_HEAD_COUNT, HD), k_blocks[index]], axis=0)
        values = jnp.concatenate([v_blocks[safe].reshape(LIST * BLK, HALF_HEAD_COUNT, HD), v_blocks[index]], axis=0)
        listed = jnp.broadcast_to(jnp.repeat(valid, BLK)[None, :], (BLK, LIST * BLK))
        mask = jnp.concatenate([listed, causal], axis=1)
        scores = jnp.einsum('thd,shd->hts', q_blocks[index].astype(jnp.float32), key_lines.astype(jnp.float32)) * HD ** (-0.5)
        scores = jnp.where(mask[None], scores, -jnp.inf)
        top = lax.optimization_barrier(jnp.max(scores, axis=-1, keepdims=True))
        probs = jnp.exp(scores - top)
        total = lax.optimization_barrier(jnp.sum(probs, axis=-1))
        rounded = probs.astype(jnp.bfloat16)
        summed = jnp.einsum('hts,shd->thd', rounded.astype(jnp.float32), values.astype(jnp.float32))
        return (summed / total.T[:, :, None]).astype(jnp.bfloat16)
    attn = lax.map(one_block, jnp.arange(NB).astype(jnp.int32)).reshape(UTTERANCE_FRAMES, width)
    branch2 = jnp.dot(attn, w_out2, preferred_element_type=jnp.float32)
    return (hidden1.astype(jnp.float32) + branch2).astype(jnp.bfloat16)
```

```python
import functools

import jax
import jax.numpy as jnp
from jax import lax
from jax.experimental import pallas as pl
from jax.experimental.pallas import tpu as pltpu
from jax.sharding import PartitionSpec as P

MESH = pl.DeviceIdType.MESH
TILE = 256
WIDE = 512
FAR = -1e30
LANES = 128
SCALE2 = 1.4426950408889634


def f32dot(a, b, dims=(((1,), (0,)), ((), ()))):
    return lax.dot_general(a, b, dims, preferred_element_type=jnp.float32)


def tile_at(index, size):
    return pl.ds(pl.multiple_of(index * size, size), size)


def norm_rows(src_ref, gain_ref, dst_ref):
    step = 128

    def body(i, carry):
        rows = tile_at(i, step)
        wide = src_ref[rows, :].astype(jnp.float32)
        scale = lax.rsqrt(jnp.mean(wide * wide, axis=-1, keepdims=True) + 1e-05)
        dst_ref[rows, :] = (wide * scale * gain_ref[...]).astype(jnp.bfloat16)
        return carry

    lax.fori_loop(0, src_ref.shape[0] // step, body, 0)


def both_layers(
    n,
    x_hbm, g1_ref, w1_hbm, ld_ref, hg_ref, wo_hbm, g2_ref, w2_hbm, ids_ref, wp_hbm,
    out_ref,
    x_ref, w1_ref, wo_ref, w2_ref, wp_ref, hid_ref, qt_ref, q_far, k_ref, v_ref,
    m_s, l_s, acc_s, s_s, o_send, o_recv, st_send, st_recv, bias_send, bias_recv,
    load_sem, kv_send, kv_recv, far_send, far_recv, bias_sems,
    h_s, qkv_s, y_s, run_s, runt_s, lin_s, x_s, ax_s, e_s, a_s, send_b, recv_b, send_sem, recv_sem,
):
    me = lax.axis_index("tm")
    rows = x_ref.shape[0]
    width = wo_ref.shape[0]
    heads = ld_ref.shape[0]
    pairs = width // LANES
    rounds = max(2, (n - 1).bit_length())
    dists = [1 << r for r in range(rounds)]

    barrier = pltpu.get_barrier_semaphore()
    for dist in dists:
        @pl.when(me + dist < n)
        def _():
            pl.semaphore_signal(barrier, inc=1, device_id={"tm": me + dist}, device_id_type=MESH)

        @pl.when(me >= dist)
        def _():
            pl.semaphore_signal(barrier, inc=1, device_id={"tm": me - dist}, device_id_type=MESH)

    loads = [
        pltpu.make_async_copy(src, dst, load_sem.at[i])
        for i, (src, dst) in enumerate(
            [
                (x_hbm, x_ref),
                (w1_hbm.at[:, width:], w1_ref.at[:, width:]),
                (w1_hbm.at[:, :width], w1_ref.at[:, :width]),
                (wo_hbm, wo_ref),
                (w2_hbm, w2_ref),
                (wp_hbm, wp_ref),
            ]
        )
    ]
    for load in loads:
        load.start()
    upper = (
        lax.broadcasted_iota(jnp.int32, (rows, rows), 0)
        <= lax.broadcasted_iota(jnp.int32, (rows, rows), 1)
    ).astype(jnp.float32)
    run = lax.dot_general(
        ld_ref[...], upper, (((1,), (0,)), ((), ())),
        precision=lax.Precision.HIGHEST, preferred_element_type=jnp.float32,
    )
    run_s[...] = run
    runt_s[...] = run.T
    last = run[:, rows - 1 : rows]
    headsel = lax.broadcasted_iota(jnp.int32, (heads, width), 1) // (
        width // heads
    ) == lax.broadcasted_iota(jnp.int32, (heads, width), 0)
    a_row = jnp.sum(jnp.where(headsel, jnp.exp(last), 0.0), axis=0, keepdims=True)
    a_s[...] = a_row
    low = lax.broadcasted_iota(jnp.int32, (1, LANES), 1) < LANES // 2
    left_t = jnp.exp(last - run).T

    loads[0].wait()
    norm_rows(x_ref, g1_ref, h_s)
    loads[1].wait()

    def project(j, carry):
        cols = tile_at(j, WIDE)
        qkv_s[:, cols] = f32dot(h_s[...], w1_ref[:, cols]).astype(jnp.bfloat16)
        return carry

    lax.fori_loop(width // WIDE, 3 * width // WIDE, project, 0)

    for p in range(pairs):
        cols = slice(p * LANES, (p + 1) * LANES)
        kcols = slice(width + p * LANES, width + (p + 1) * LANES)
        vcols = slice(2 * width + p * LANES, 2 * width + (p + 1) * LANES)
        decay = jnp.where(low, left_t[:, 2 * p : 2 * p + 1], left_t[:, 2 * p + 1 : 2 * p + 2])
        keyed = (qkv_s[:, kcols].astype(jnp.float32) * decay).T.astype(jnp.bfloat16)
        full = f32dot(keyed, qkv_s[:, vcols])
        e_s[:, cols] = jnp.where(low, full[: LANES // 2], full[LANES // 2 :])
    x_s[...] = jnp.zeros_like(x_s)
    ax_s[...] = jnp.ones_like(ax_s)

    def send(r, dist):
        w = e_s[...] + a_s[...] * x_s[...]
        aw = a_s[...] * ax_s[...]
        hi = aw.astype(jnp.bfloat16).astype(jnp.float32)
        lo = aw - hi
        row = lax.broadcasted_iota(jnp.int32, (16, width), 0)
        tail = jnp.where(row == 0, hi, jnp.where(row == 1, lo, 0.0))
        send_b[r, 0:64, :] = w.astype(jnp.bfloat16)
        send_b[r, 64:80, :] = tail.astype(jnp.bfloat16)

        @pl.when(me + dist < n)
        def _():
            copy_of(r, dist).start()

    def copy_of(r, dist):
        return pltpu.make_async_remote_copy(
            src_ref=send_b.at[r], dst_ref=recv_b.at[r],
            send_sem=send_sem.at[r], recv_sem=recv_sem.at[r],
            device_id={"tm": me + dist}, device_id_type=MESH,
        )

    def receive(r, dist):
        @pl.when(me >= dist)
        def _():
            copy_of(r, dist).wait_recv()
            got = recv_b[r].astype(jnp.float32)
            x_s[...] = x_s[...] + ax_s[...] * got[0:64]
            ax_s[...] = ax_s[...] * (got[64:65] + got[65:66])

    peers = [me + dist < n for dist in dists] + [me >= dist for dist in dists]
    pl.semaphore_wait(barrier, sum(peer.astype(jnp.int32) for peer in peers))

    core = lax.rem(me, 2)
    even = core == 0
    odd = jnp.logical_not(even)
    helps = me + 2 < n
    helped = me >= 2
    hands_on = jnp.logical_and(odd, me + 3 < n)
    gets_prev = jnp.logical_and(even, jnp.logical_and(me >= 2, helps))

    def listing(back):
        listed = ids_ref[0, 0] == me - back
        for j in range(1, ids_ref.shape[1]):
            listed = jnp.logical_or(listed, ids_ref[0, j] == me - back)
        return jnp.where(listed, jnp.float32(0.0), jnp.float32(FAR))

    def bias_back():
        return pltpu.make_async_remote_copy(
            src_ref=bias_send, dst_ref=bias_recv,
            send_sem=bias_sems.at[0], recv_sem=bias_sems.at[1],
            device_id={"tm": me - 2}, device_id_type=MESH,
        )

    near = jnp.where(even, listing(1), listing(3))
    brow = lax.broadcasted_iota(jnp.int32, bias_send.shape, 0)
    bias_send[...] = jnp.where(brow == 0, listing(2), jnp.where(brow == 1, near, listing(3)))

    @pl.when(helped)
    def _():
        bias_back().start()

    def work_query():
        loads[2].wait()
        lax.fori_loop(0, width // WIDE, project, 0)

    def work_pair(p):
        cols = slice(p * LANES, (p + 1) * LANES)
        kcols = slice(width + p * LANES, width + (p + 1) * LANES)
        vcols = slice(2 * width + p * LANES, 2 * width + (p + 1) * LANES)
        for first in range(0, rows, TILE):
            upto = first + TILE
            parts = []
            query = qkv_s[first:upto, cols]
            keys = qkv_s[0:upto, kcols]
            vals = qkv_s[0:upto, vcols]
            causal = lax.broadcasted_iota(jnp.int32, (TILE, upto), 0) + first >= (
                lax.broadcasted_iota(jnp.int32, (TILE, upto), 1)
            )
            for half in range(2):
                h = 2 * p + half
                keep = low if half == 0 else jnp.logical_not(low)
                mine = jnp.where(keep, query.astype(jnp.float32), 0.0).astype(jnp.bfloat16)
                scores = f32dot(mine, keys, (((1,), (1,)), ((), ())))
                diff = runt_s[first:upto, h : h + 1] - run_s[h : h + 1, 0:upto]
                weight = jnp.where(causal, jnp.exp(jnp.minimum(diff, 0.0)), 0.0)
                parts.append(f32dot((scores * weight).astype(jnp.bfloat16), vals))
            lin_s[first:upto, cols] = jnp.where(low, parts[0], parts[1])

    work = [work_query] + [functools.partial(work_pair, p) for p in range(pairs)]
    send(0, dists[0])
    for r, dist in enumerate(dists):
        take = 1 if r < rounds - 1 else len(work)
        if r == 1:
            take = 2
        for item in work[:take]:
            item()
        work = work[take:]
        receive(r, dist)
        if r + 1 < rounds:
            send(r + 1, dists[r + 1])
    for item in work:
        item()

    for p in range(pairs):
        cols = slice(p * LANES, (p + 1) * LANES)
        packed = x_s[:, cols]
        state = jnp.concatenate(
            [jnp.where(low, packed, 0.0), jnp.where(low, 0.0, packed)], axis=0
        ).astype(jnp.bfloat16)
        grow = jnp.exp(
            jnp.where(low, runt_s[:, 2 * p : 2 * p + 1], runt_s[:, 2 * p + 1 : 2 * p + 2])
        )
        scaled = (qkv_s[:, cols].astype(jnp.float32) * grow).astype(jnp.bfloat16)
        lin = lin_s[:, cols] + f32dot(scaled, state)
        square = lin * lin
        s0 = jnp.sum(jnp.where(low, square, 0.0), axis=-1, keepdims=True)
        s1 = jnp.sum(jnp.where(low, 0.0, square), axis=-1, keepdims=True)
        mean = jnp.where(low, s0, s1) * (1.0 / 64)
        y_s[:, cols] = (lin * lax.rsqrt(mean + 1e-06) * hg_ref[:, cols]).astype(jnp.bfloat16)

    def out_tile(j, carry):
        cols = tile_at(j, WIDE)
        branch = f32dot(y_s[...], wo_ref[:, cols])
        hid_ref[:, cols] = (x_ref[:, cols].astype(jnp.float32) + branch).astype(jnp.bfloat16)
        return carry

    loads[3].wait()
    lax.fori_loop(0, x_ref.shape[1] // WIDE, out_tile, 0)
    loads[4].wait()
    norm_rows(hid_ref, g2_ref, h_s)

    def query_back(p):
        return pltpu.make_async_remote_copy(
            src_ref=qt_ref.at[p], dst_ref=q_far.at[p],
            send_sem=far_send.at[p, 0], recv_sem=far_recv.at[p, 0],
            device_id={"tm": me - 2}, device_id_type=MESH,
        )

    def partial_on(p):
        return [
            pltpu.make_async_remote_copy(
                src_ref=src.at[p], dst_ref=dst.at[p],
                send_sem=far_send.at[p, i], recv_sem=far_recv.at[p, i],
                device_id={"tm": me + 2}, device_id_type=MESH,
            )
            for i, (src, dst) in [(1, (o_send, o_recv)), (2, (st_send, st_recv))]
        ]

    def kv_to(slot, shift):
        return [
            pltpu.make_async_remote_copy(
                src_ref=ref.at[0], dst_ref=ref.at[slot],
                send_sem=kv_send.at[slot - 1, i], recv_sem=kv_recv.at[slot - 1, i],
                device_id={"tm": me + shift}, device_id_type=MESH,
            )
            for i, ref in enumerate([k_ref, v_ref])
        ]

    to_sib = 1 - 2 * core
    sib, on = kv_to(1, to_sib), kv_to(2, 1)

    block = f32dot(h_s[...], w2_ref[:, 0:width]) * (SCALE2 * 64 ** (-0.5))
    for p in range(pairs):
        qt_ref[p] = block[:, p * LANES : (p + 1) * LANES].T.astype(jnp.bfloat16)

        @pl.when(helped)
        def _():
            query_back(p).start()

    block = f32dot(h_s[...], w2_ref[:, width : 2 * width]).astype(jnp.bfloat16)
    for p in range(pairs):
        k_ref[0, p] = block[:, p * LANES : (p + 1) * LANES]
    sib[0].start()

    @pl.when(hands_on)
    def _():
        on[0].start()

    block = f32dot(h_s[...], w2_ref[:, 2 * width : 3 * width])
    for p in range(pairs):
        v_ref[0, p] = block[:, p * LANES : (p + 1) * LANES].T.astype(jnp.bfloat16)
    sib[1].start()

    @pl.when(hands_on)
    def _():
        on[1].start()

    half_rows = LANES // 2
    blank = jnp.zeros((half_rows, rows), jnp.bfloat16)

    def pair_attend(p, query, slots, biases, diag, put):
        def score(half):
            own = query[half * half_rows : (half + 1) * half_rows, :]
            mine = jnp.concatenate([own, blank] if half == 0 else [blank, own], axis=0)
            tops = []
            for j, slot in enumerate(slots):
                s = f32dot(k_ref[slot, p], mine)
                if diag:
                    seen = lax.broadcasted_iota(jnp.int32, s.shape, 0) <= (
                        lax.broadcasted_iota(jnp.int32, s.shape, 1)
                    )
                    s = jnp.where(seen, s, FAR)
                s_s[half * 3 + j] = s
                tops.append(jnp.max(s, axis=0, keepdims=True))
            if biases is None:
                return tops[0], tops
            best = functools.reduce(
                jnp.maximum, [top + bias for top, bias in zip(tops, biases)]
            )
            return best, [jnp.maximum(best - bias, top) for top, bias in zip(tops, biases)]

        def soft(half, best, refs):
            total, acc = None, None
            for j, slot in enumerate(slots):
                w = jnp.exp2(s_s[half * 3 + j] - refs[j])
                add = jnp.sum(w, axis=0, keepdims=True)
                part = f32dot(
                    v_ref[slot, p, half * half_rows : (half + 1) * half_rows, :],
                    w.astype(jnp.bfloat16),
                )
                total = add if total is None else total + add
                acc = part if acc is None else acc + part
            put(p, half, best, total, acc)

        first = score(0)
        second = score(1)
        soft(0, *first)
        soft(1, *second)

    def put_own(p, half, best, total, acc):
        m_s[p, half] = best
        l_s[p, half] = total
        acc_s[p, half * half_rows : (half + 1) * half_rows, :] = acc

    def put_merged(p, half, best, total, acc):
        arow = slice(half * half_rows, (half + 1) * half_rows)
        m_old = m_s[p, half]
        m_new = jnp.maximum(m_old, best)
        alpha, beta = jnp.exp2(m_old - m_new), jnp.exp2(best - m_new)
        m_s[p, half] = m_new
        l_s[p, half] = l_s[p, half] * alpha + total * beta
        acc_s[p, arow, :] = acc_s[p, arow, :] * alpha + acc * beta

    def put_far(p, half, best, total, acc):
        st_send[p, half : half + 1, :] = best
        st_send[p, half + 2 : half + 3, :] = total
        o_send[p, half * half_rows : (half + 1) * half_rows, :] = acc.astype(jnp.bfloat16)

    def loop_pairs(body):
        def step(p, carry):
            body(p)
            return carry

        lax.fori_loop(0, pairs, step, 0)

    loop_pairs(lambda p: pair_attend(p, qt_ref[p], [0], None, True, put_own))
    for copy in sib:
        copy.wait_recv()

    @pl.when(odd)
    def _():
        bias = listing(1)
        loop_pairs(lambda p: pair_attend(p, qt_ref[p], [1], [bias], False, put_merged))

    @pl.when(helps)
    def _():
        bias_back().wait_recv()

    def help_with(slots):
        biases = [bias_recv[j : j + 1, 0:1] for j in range(len(slots))]

        def body(p):
            query_back(p).wait_recv()
            pair_attend(p, q_far[p], slots, biases, False, put_far)
            for copy in partial_on(p):
                copy.start()

        loop_pairs(body)

    @pl.when(gets_prev)
    def _():
        for copy in on:
            copy.wait_recv()
        help_with([0, 1, 2])

    @pl.when(jnp.logical_and(helps, jnp.logical_not(gets_prev)))
    def _():
        help_with([0, 1])

    for p in range(pairs):
        @pl.when(helped)
        def _():
            for copy in partial_on(p):
                copy.wait_recv()
            for half in range(2):
                far = o_recv[p, half * half_rows : (half + 1) * half_rows, :]
                put_merged(
                    p, half, st_recv[p, half : half + 1, :],
                    st_recv[p, half + 2 : half + 3, :], far.astype(jnp.float32),
                )

        whole = jnp.concatenate(
            [
                acc_s[p, 0:half_rows, :] * (1.0 / l_s[p, 0]),
                acc_s[p, half_rows:LANES, :] * (1.0 / l_s[p, 1]),
            ],
            axis=0,
        )
        y_s[:, p * LANES : (p + 1) * LANES] = whole.T.astype(jnp.bfloat16)

    def last_tile(j, carry):
        cols = tile_at(j, WIDE)
        branch = f32dot(y_s[...], wp_ref[:, cols])
        out_ref[:, cols] = (hid_ref[:, cols].astype(jnp.float32) + branch).astype(jnp.bfloat16)
        return carry

    loads[5].wait()
    lax.fori_loop(0, hid_ref.shape[1] // WIDE, last_tile, 0)

    def drain(copies):
        for copy in copies:
            copy.wait_send()

    for r, dist in enumerate(dists):
        @pl.when(me + dist < n)
        def _():
            copy_of(r, dist).wait_send()

    drain(sib)

    @pl.when(hands_on)
    def _():
        drain(on)

    @pl.when(helped)
    def _():
        drain([bias_back()])

    for p in range(pairs):
        @pl.when(helped)
        def _():
            drain([query_back(p)])

        @pl.when(helps)
        def _():
            drain(partial_on(p))


def local(
    frames, norm_gain1, w_qkv1, log_decay, head_gain, w_out1, norm_gain2, w_qkv2, window_ids, w_out2
):
    n = lax.axis_size("tm")
    rows, model = frames.shape
    width = w_out1.shape[0]
    heads = log_decay.shape[0]
    rounds = max(2, (n - 1).bit_length())
    pairs = width // LANES
    vmem = pl.BlockSpec(memory_space=pltpu.VMEM)
    hbm = pl.BlockSpec(memory_space=pltpu.HBM)
    smem = pl.BlockSpec(memory_space=pltpu.SMEM)
    bf, f32 = jnp.bfloat16, jnp.float32
    return pl.pallas_call(
        functools.partial(both_layers, n),
        out_shape=jax.ShapeDtypeStruct((rows, model), bf),
        in_specs=[hbm, vmem, hbm, vmem, vmem, hbm, vmem, hbm, smem, hbm],
        out_specs=vmem,
        scratch_shapes=[
            pltpu.VMEM((rows, model), bf),
            pltpu.VMEM((model, 3 * width), bf),
            pltpu.VMEM((width, model), bf),
            pltpu.VMEM((model, 3 * width), bf),
            pltpu.VMEM((width, model), bf),
            pltpu.VMEM((rows, model), bf),
            pltpu.VMEM((pairs, LANES, rows), bf),
            pltpu.VMEM((pairs, LANES, rows), bf),
            pltpu.VMEM((3, pairs, rows, LANES), bf),
            pltpu.VMEM((3, pairs, LANES, rows), bf),
            pltpu.VMEM((pairs, 2, 1, rows), f32),
            pltpu.VMEM((pairs, 2, 1, rows), f32),
            pltpu.VMEM((pairs, LANES, rows), f32),
            pltpu.VMEM((6, rows, rows), f32),
            pltpu.VMEM((pairs, LANES, rows), bf),
            pltpu.VMEM((pairs, LANES, rows), bf),
            pltpu.VMEM((pairs, 8, rows), f32),
            pltpu.VMEM((pairs, 8, rows), f32),
            pltpu.VMEM((8, LANES), f32),
            pltpu.VMEM((8, LANES), f32),
            pltpu.SemaphoreType.DMA((6,)),
            pltpu.SemaphoreType.DMA((2, 2)),
            pltpu.SemaphoreType.DMA((2, 2)),
            pltpu.SemaphoreType.DMA((pairs, 3)),
            pltpu.SemaphoreType.DMA((pairs, 3)),
            pltpu.SemaphoreType.DMA((2,)),
            pltpu.VMEM((rows, model), bf),
            pltpu.VMEM((rows, 3 * width), bf),
            pltpu.VMEM((rows, width), bf),
            pltpu.VMEM((heads, rows), f32),
            pltpu.VMEM((rows, heads), f32),
            pltpu.VMEM((rows, width), f32),
            pltpu.VMEM((64, width), f32),
            pltpu.VMEM((1, width), f32),
            pltpu.VMEM((64, width), f32),
            pltpu.VMEM((1, width), f32),
            pltpu.VMEM((rounds, 80, width), bf),
            pltpu.VMEM((rounds, 80, width), bf),
            pltpu.SemaphoreType.DMA((rounds,)),
            pltpu.SemaphoreType.DMA((rounds,)),
        ],
        compiler_params=pltpu.CompilerParams(
            collective_id=0, has_side_effects=True, vmem_limit_bytes=60 * 2**20
        ),
    )(
        frames, norm_gain1.reshape(1, model), w_qkv1, log_decay, head_gain.reshape(1, width),
        w_out1, norm_gain2.reshape(1, model), w_qkv2, window_ids, w_out2,
    )


def solution(mesh):
    placed = (
        P(("dp", "tm"), None),
        P(),
        P(),
        P(None, ("dp", "tm")),
        P(),
        P(),
        P(),
        P(),
        P(("dp", "tm"), None),
        P(),
    )
    return jax.shard_map(
        local, mesh=mesh, in_specs=placed, out_specs=P(("dp", "tm"), None), check_vma=False
    )
```

```python
import functools

import jax
import jax.numpy as jnp
from jax import lax
from jax.experimental import pallas as pl
from jax.experimental.pallas import tpu as pltpu
from jax.sharding import PartitionSpec as P

MESH = pl.DeviceIdType.MESH
TILE = 256
WIDE = 512
FAR = -1e30
LANES = 128
SCALE2 = 1.4426950408889634


def f32dot(a, b, dims=(((1,), (0,)), ((), ()))):
    return lax.dot_general(a, b, dims, preferred_element_type=jnp.float32)


def tile_at(index, size):
    return pl.ds(pl.multiple_of(index * size, size), size)


def norm_rows(src_ref, gain_ref, dst_ref):
    step = 128

    def body(i, carry):
        rows = tile_at(i, step)
        wide = src_ref[rows, :].astype(jnp.float32)
        scale = lax.rsqrt(jnp.mean(wide * wide, axis=-1, keepdims=True) + 1e-05)
        dst_ref[rows, :] = (wide * scale * gain_ref[...]).astype(jnp.bfloat16)
        return carry

    lax.fori_loop(0, src_ref.shape[0] // step, body, 0)


def both_layers(
    n,
    x_hbm, g1_ref, w1_hbm, ld_ref, hg_ref, wo_hbm, g2_ref, w2_hbm, ids_ref,
    y_out, hid_ref,
    x_ref, w1_ref, wo_ref, w2_ref, qt_ref, q_far, k_ref, v_ref,
    m_s, l_s, acc_s, fm_s, fl_s, facc_s, s_s, o_send, o_recv, st_send, st_recv, bias_send, bias_recv,
    load_sem, kv_send, kv_recv, far_send, far_recv, bias_sems,
    h_s, qkv_s, y_s, run_s, runt_s, lin_s, x_s, ax_s, e_s, a_s, send_b, recv_b, send_sem, recv_sem,
):
    me = lax.axis_index("tm")
    rows = x_ref.shape[0]
    width = wo_ref.shape[0]
    heads = ld_ref.shape[0]
    pairs = width // LANES
    rounds = max(2, (n - 1).bit_length())
    dists = [1 << r for r in range(rounds)]

    barrier = pltpu.get_barrier_semaphore()
    for dist in dists:
        @pl.when(me + dist < n)
        def _():
            pl.semaphore_signal(barrier, inc=1, device_id={"tm": me + dist}, device_id_type=MESH)

        @pl.when(me >= dist)
        def _():
            pl.semaphore_signal(barrier, inc=1, device_id={"tm": me - dist}, device_id_type=MESH)

    loads = [
        pltpu.make_async_copy(src, dst, load_sem.at[i])
        for i, (src, dst) in enumerate(
            [
                (x_hbm, x_ref),
                (w1_hbm.at[:, width:], w1_ref.at[:, width:]),
                (w1_hbm.at[:, :width], w1_ref.at[:, :width]),
                (wo_hbm, wo_ref),
                (w2_hbm, w2_ref),
            ]
        )
    ]
    for load in loads:
        load.start()
    upper = (
        lax.broadcasted_iota(jnp.int32, (rows, rows), 0)
        <= lax.broadcasted_iota(jnp.int32, (rows, rows), 1)
    ).astype(jnp.float32)
    run = lax.dot_general(
        ld_ref[...], upper, (((1,), (0,)), ((), ())),
        precision=lax.Precision.HIGHEST, preferred_element_type=jnp.float32,
    )
    run_s[...] = run
    runt_s[...] = run.T
    last = run[:, rows - 1 : rows]
    headsel = lax.broadcasted_iota(jnp.int32, (heads, width), 1) // (
        width // heads
    ) == lax.broadcasted_iota(jnp.int32, (heads, width), 0)
    a_row = jnp.sum(jnp.where(headsel, jnp.exp(last), 0.0), axis=0, keepdims=True)
    a_s[...] = a_row
    low = lax.broadcasted_iota(jnp.int32, (1, LANES), 1) < LANES // 2
    left_t = jnp.exp(last - run).T

    loads[0].wait()
    norm_rows(x_ref, g1_ref, h_s)
    loads[1].wait()

    def project(j, carry):
        cols = tile_at(j, WIDE)
        qkv_s[:, cols] = f32dot(h_s[...], w1_ref[:, cols]).astype(jnp.bfloat16)
        return carry

    lax.fori_loop(width // WIDE, 3 * width // WIDE, project, 0)

    for p in range(pairs):
        cols = slice(p * LANES, (p + 1) * LANES)
        kcols = slice(width + p * LANES, width + (p + 1) * LANES)
        vcols = slice(2 * width + p * LANES, 2 * width + (p + 1) * LANES)
        decay = jnp.where(low, left_t[:, 2 * p : 2 * p + 1], left_t[:, 2 * p + 1 : 2 * p + 2])
        keyed = (qkv_s[:, kcols].astype(jnp.float32) * decay).T.astype(jnp.bfloat16)
        full = f32dot(keyed, qkv_s[:, vcols])
        e_s[:, cols] = jnp.where(low, full[: LANES // 2], full[LANES // 2 :])
    x_s[...] = jnp.zeros_like(x_s)
    ax_s[...] = jnp.ones_like(ax_s)

    def send(r, dist):
        w = e_s[...] + a_s[...] * x_s[...]
        aw = a_s[...] * ax_s[...]
        hi = aw.astype(jnp.bfloat16).astype(jnp.float32)
        lo = aw - hi
        row = lax.broadcasted_iota(jnp.int32, (16, width), 0)
        tail = jnp.where(row == 0, hi, jnp.where(row == 1, lo, 0.0))
        send_b[r, 0:64, :] = w.astype(jnp.bfloat16)
        send_b[r, 64:80, :] = tail.astype(jnp.bfloat16)

        @pl.when(me + dist < n)
        def _():
            copy_of(r, dist).start()

    def copy_of(r, dist):
        return pltpu.make_async_remote_copy(
            src_ref=send_b.at[r], dst_ref=recv_b.at[r],
            send_sem=send_sem.at[r], recv_sem=recv_sem.at[r],
            device_id={"tm": me + dist}, device_id_type=MESH,
        )

    def receive(r, dist):
        @pl.when(me >= dist)
        def _():
            copy_of(r, dist).wait_recv()
            got = recv_b[r].astype(jnp.float32)
            x_s[...] = x_s[...] + ax_s[...] * got[0:64]
            ax_s[...] = ax_s[...] * (got[64:65] + got[65:66])

    peers = [me + dist < n for dist in dists] + [me >= dist for dist in dists]
    pl.semaphore_wait(barrier, sum(peer.astype(jnp.int32) for peer in peers))

    core = lax.rem(me, 2)
    even = core == 0
    odd = jnp.logical_not(even)
    helps = me + 2 < n
    helped = me >= 2
    hands_on = jnp.logical_and(odd, me + 3 < n)
    gets_prev = jnp.logical_and(even, jnp.logical_and(me >= 2, helps))

    def listing(back):
        listed = ids_ref[0, 0] == me - back
        for j in range(1, ids_ref.shape[1]):
            listed = jnp.logical_or(listed, ids_ref[0, j] == me - back)
        return jnp.where(listed, jnp.float32(0.0), jnp.float32(FAR))

    def bias_back():
        return pltpu.make_async_remote_copy(
            src_ref=bias_send, dst_ref=bias_recv,
            send_sem=bias_sems.at[0], recv_sem=bias_sems.at[1],
            device_id={"tm": me - 2}, device_id_type=MESH,
        )

    near = jnp.where(even, listing(1), listing(3))
    brow = lax.broadcasted_iota(jnp.int32, bias_send.shape, 0)
    bias_send[...] = jnp.where(brow == 0, listing(2), jnp.where(brow == 1, near, listing(3)))

    @pl.when(helped)
    def _():
        bias_back().start()

    def work_query():
        loads[2].wait()
        lax.fori_loop(0, width // WIDE, project, 0)

    def work_pair(p):
        cols = slice(p * LANES, (p + 1) * LANES)
        kcols = slice(width + p * LANES, width + (p + 1) * LANES)
        vcols = slice(2 * width + p * LANES, 2 * width + (p + 1) * LANES)
        for first in range(0, rows, TILE):
            upto = first + TILE
            parts = []
            query = qkv_s[first:upto, cols]
            keys = qkv_s[0:upto, kcols]
            vals = qkv_s[0:upto, vcols]
            causal = lax.broadcasted_iota(jnp.int32, (TILE, upto), 0) + first >= (
                lax.broadcasted_iota(jnp.int32, (TILE, upto), 1)
            )
            for half in range(2):
                h = 2 * p + half
                keep = low if half == 0 else jnp.logical_not(low)
                mine = jnp.where(keep, query.astype(jnp.float32), 0.0).astype(jnp.bfloat16)
                scores = f32dot(mine, keys, (((1,), (1,)), ((), ())))
                diff = runt_s[first:upto, h : h + 1] - run_s[h : h + 1, 0:upto]
                weight = jnp.where(causal, jnp.exp(jnp.minimum(diff, 0.0)), 0.0)
                parts.append(f32dot((scores * weight).astype(jnp.bfloat16), vals))
            lin_s[first:upto, cols] = jnp.where(low, parts[0], parts[1])

    work = [work_query] + [functools.partial(work_pair, p) for p in range(pairs)]
    send(0, dists[0])
    for r, dist in enumerate(dists):
        take = 1 if r < rounds - 1 else len(work)
        if r == 1:
            take = 2
        for item in work[:take]:
            item()
        work = work[take:]
        receive(r, dist)
        if r + 1 < rounds:
            send(r + 1, dists[r + 1])
    for item in work:
        item()

    for p in range(pairs):
        cols = slice(p * LANES, (p + 1) * LANES)
        packed = x_s[:, cols]
        state = jnp.concatenate(
            [jnp.where(low, packed, 0.0), jnp.where(low, 0.0, packed)], axis=0
        ).astype(jnp.bfloat16)
        grow = jnp.exp(
            jnp.where(low, runt_s[:, 2 * p : 2 * p + 1], runt_s[:, 2 * p + 1 : 2 * p + 2])
        )
        scaled = (qkv_s[:, cols].astype(jnp.float32) * grow).astype(jnp.bfloat16)
        lin = lin_s[:, cols] + f32dot(scaled, state)
        square = lin * lin
        s0 = jnp.sum(jnp.where(low, square, 0.0), axis=-1, keepdims=True)
        s1 = jnp.sum(jnp.where(low, 0.0, square), axis=-1, keepdims=True)
        mean = jnp.where(low, s0, s1) * (1.0 / 64)
        y_s[:, cols] = (lin * lax.rsqrt(mean + 1e-06) * hg_ref[:, cols]).astype(jnp.bfloat16)

    def out_tile(j, carry):
        cols = tile_at(j, WIDE)
        branch = f32dot(y_s[...], wo_ref[:, cols])
        hid_ref[:, cols] = (x_ref[:, cols].astype(jnp.float32) + branch).astype(jnp.bfloat16)
        return carry

    loads[3].wait()
    lax.fori_loop(0, x_ref.shape[1] // WIDE, out_tile, 0)
    loads[4].wait()
    norm_rows(hid_ref, g2_ref, h_s)

    def query_back(p):
        return pltpu.make_async_remote_copy(
            src_ref=qt_ref.at[p], dst_ref=q_far.at[p],
            send_sem=far_send.at[p, 0], recv_sem=far_recv.at[p, 0],
            device_id={"tm": me - 2}, device_id_type=MESH,
        )

    def partial_on(p):
        return [
            pltpu.make_async_remote_copy(
                src_ref=src.at[p], dst_ref=dst.at[p],
                send_sem=far_send.at[p, i], recv_sem=far_recv.at[p, i],
                device_id={"tm": me + 2}, device_id_type=MESH,
            )
            for i, (src, dst) in [(1, (o_send, o_recv)), (2, (st_send, st_recv))]
        ]

    def kv_to(slot, shift):
        return [
            pltpu.make_async_remote_copy(
                src_ref=ref.at[0], dst_ref=ref.at[slot],
                send_sem=kv_send.at[slot - 1, i], recv_sem=kv_recv.at[slot - 1, i],
                device_id={"tm": me + shift}, device_id_type=MESH,
            )
            for i, ref in enumerate([k_ref, v_ref])
        ]

    to_sib = 1 - 2 * core
    sib, on = kv_to(1, to_sib), kv_to(2, 1)

    block = f32dot(h_s[...], w2_ref[:, 0:width]) * (SCALE2 * 64 ** (-0.5))
    for p in range(pairs):
        qt_ref[p] = block[:, p * LANES : (p + 1) * LANES].T.astype(jnp.bfloat16)

        @pl.when(helped)
        def _():
            query_back(p).start()

    block = f32dot(h_s[...], w2_ref[:, width : 2 * width]).astype(jnp.bfloat16)
    for p in range(pairs):
        k_ref[0, p] = block[:, p * LANES : (p + 1) * LANES]
    sib[0].start()

    @pl.when(hands_on)
    def _():
        on[0].start()

    block = f32dot(h_s[...], w2_ref[:, 2 * width : 3 * width])
    for p in range(pairs):
        v_ref[0, p] = block[:, p * LANES : (p + 1) * LANES].T.astype(jnp.bfloat16)
    sib[1].start()

    @pl.when(hands_on)
    def _():
        on[1].start()

    half_rows = LANES // 2
    blank = jnp.zeros((half_rows, rows), jnp.bfloat16)

    def pair_attend(p, query, slots, biases, diag, put):
        def score(half):
            own = query[half * half_rows : (half + 1) * half_rows, :]
            mine = jnp.concatenate([own, blank] if half == 0 else [blank, own], axis=0)
            tops = []
            for j, slot in enumerate(slots):
                s = f32dot(k_ref[slot, p], mine)
                if diag:
                    seen = lax.broadcasted_iota(jnp.int32, s.shape, 0) <= (
                        lax.broadcasted_iota(jnp.int32, s.shape, 1)
                    )
                    s = jnp.where(seen, s, FAR)
                s_s[half * 3 + j] = s
                tops.append(jnp.max(s, axis=0, keepdims=True))
            if biases is None:
                return tops[0], tops
            best = functools.reduce(
                jnp.maximum, [top + bias for top, bias in zip(tops, biases)]
            )
            return best, [jnp.maximum(best - bias, top) for top, bias in zip(tops, biases)]

        def soft(half, best, refs):
            total, acc = None, None
            for j, slot in enumerate(slots):
                w = jnp.exp2(s_s[half * 3 + j] - refs[j])
                add = jnp.sum(w, axis=0, keepdims=True)
                part = f32dot(
                    v_ref[slot, p, half * half_rows : (half + 1) * half_rows, :],
                    w.astype(jnp.bfloat16),
                )
                total = add if total is None else total + add
                acc = part if acc is None else acc + part
            put(p, half, best, total, acc)

        first = score(0)
        second = score(1)
        soft(0, *first)
        soft(1, *second)

    def put_own(p, half, best, total, acc):
        m_s[p, half] = best
        l_s[p, half] = total
        acc_s[p, half * half_rows : (half + 1) * half_rows, :] = acc

    def put_merged(p, half, best, total, acc):
        arow = slice(half * half_rows, (half + 1) * half_rows)
        m_old = m_s[p, half]
        m_new = jnp.maximum(m_old, best)
        alpha, beta = jnp.exp2(m_old - m_new), jnp.exp2(best - m_new)
        m_s[p, half] = m_new
        l_s[p, half] = l_s[p, half] * alpha + total * beta
        acc_s[p, arow, :] = acc_s[p, arow, :] * alpha + acc * beta

    def put_far(p, half, best, total, acc):
        st_send[p, half : half + 1, :] = best
        st_send[p, half + 2 : half + 3, :] = total
        o_send[p, half * half_rows : (half + 1) * half_rows, :] = acc.astype(jnp.bfloat16)

    def loop_pairs(body):
        def step(p, carry):
            body(p)
            return carry

        lax.fori_loop(0, pairs, step, 0)

    def put_part(p, half, best, total, acc):
        fm_s[p, half] = best
        fl_s[p, half] = total
        facc_s[p, half * half_rows : (half + 1) * half_rows, :] = acc

    def put_last(p, half, best, total, acc):
        arow = slice(half * half_rows, (half + 1) * half_rows)
        m_old = fm_s[p, half]
        m_new = jnp.maximum(m_old, best)
        alpha, beta = jnp.exp2(m_old - m_new), jnp.exp2(best - m_new)
        put_far(
            p, half, m_new, fl_s[p, half] * alpha + total * beta,
            facc_s[p, arow, :] * alpha + acc * beta,
        )

    loop_pairs(lambda p: pair_attend(p, qt_ref[p], [0], None, True, put_own))
    for copy in sib:
        copy.wait_recv()

    def help_bias(j):
        return bias_recv[j : j + 1, 0:1]

    def give(p):
        for copy in partial_on(p):
            copy.start()

    def near_part(p, put):
        query_back(p).wait_recv()
        pair_attend(p, q_far[p], [0, 1], [help_bias(0), help_bias(1)], False, put)

    @pl.when(helps)
    def _():
        bias_back().wait_recv()

    @pl.when(gets_prev)
    def _():
        loop_pairs(lambda p: near_part(p, put_part))
        for copy in on:
            copy.wait_recv()

        def body(p):
            pair_attend(p, q_far[p], [2], [help_bias(2)], False, put_last)
            give(p)

        loop_pairs(body)

    @pl.when(jnp.logical_and(helps, jnp.logical_not(gets_prev)))
    def _():
        def body(p):
            near_part(p, put_far)
            give(p)

        loop_pairs(body)

    @pl.when(odd)
    def _():
        bias = listing(1)
        loop_pairs(lambda p: pair_attend(p, qt_ref[p], [1], [bias], False, put_merged))

    for p in range(pairs):
        @pl.when(helped)
        def _():
            for copy in partial_on(p):
                copy.wait_recv()
            for half in range(2):
                far = o_recv[p, half * half_rows : (half + 1) * half_rows, :]
                put_merged(
                    p, half, st_recv[p, half : half + 1, :],
                    st_recv[p, half + 2 : half + 3, :], far.astype(jnp.float32),
                )

        whole = jnp.concatenate(
            [
                acc_s[p, 0:half_rows, :] * (1.0 / l_s[p, 0]),
                acc_s[p, half_rows:LANES, :] * (1.0 / l_s[p, 1]),
            ],
            axis=0,
        )
        y_out[:, p * LANES : (p + 1) * LANES] = whole.T.astype(jnp.bfloat16)

    def drain(copies):
        for copy in copies:
            copy.wait_send()

    for r, dist in enumerate(dists):
        @pl.when(me + dist < n)
        def _():
            copy_of(r, dist).wait_send()

    drain(sib)

    @pl.when(hands_on)
    def _():
        drain(on)

    @pl.when(helped)
    def _():
        drain([bias_back()])

    for p in range(pairs):
        @pl.when(helped)
        def _():
            drain([query_back(p)])

        @pl.when(helps)
        def _():
            drain(partial_on(p))


def close_layer(y_ref, hid_ref, wp_ref, out_hbm, out_ref, sems):
    copies = []
    for i in range(out_ref.shape[0] // LANES):
        rows = slice(i * LANES, (i + 1) * LANES)
        branch = f32dot(y_ref[rows, :], wp_ref[...])
        out_ref[rows, :] = (hid_ref[rows, :].astype(jnp.float32) + branch).astype(jnp.bfloat16)
        copies.append(pltpu.make_async_copy(out_ref.at[rows], out_hbm.at[rows], sems.at[i]))
        copies[-1].start()
    for copy in copies:
        copy.wait()


def in_vmem(array):
    return pltpu.with_memory_space_constraint(array, pltpu.VMEM)


def local(
    frames, norm_gain1, w_qkv1, log_decay, head_gain, w_out1, norm_gain2, w_qkv2, window_ids, w_out2
):
    n = lax.axis_size("tm")
    rows, model = frames.shape
    width = w_out1.shape[0]
    heads = log_decay.shape[0]
    rounds = max(2, (n - 1).bit_length())
    pairs = width // LANES
    vmem = pl.BlockSpec(memory_space=pltpu.VMEM)
    hbm = pl.BlockSpec(memory_space=pltpu.HBM)
    smem = pl.BlockSpec(memory_space=pltpu.SMEM)
    bf, f32 = jnp.bfloat16, jnp.float32
    y, hid = pl.pallas_call(
        functools.partial(both_layers, n),
        out_shape=[
            pltpu.VMEM((rows, width), bf),
            pltpu.VMEM((rows, model), bf),
        ],
        in_specs=[hbm, vmem, hbm, vmem, vmem, hbm, vmem, hbm, smem],
        out_specs=[vmem, vmem],
        scratch_shapes=[
            pltpu.VMEM((rows, model), bf),
            pltpu.VMEM((model, 3 * width), bf),
            pltpu.VMEM((width, model), bf),
            pltpu.VMEM((model, 3 * width), bf),
            pltpu.VMEM((pairs, LANES, rows), bf),
            pltpu.VMEM((pairs, LANES, rows), bf),
            pltpu.VMEM((3, pairs, rows, LANES), bf),
            pltpu.VMEM((3, pairs, LANES, rows), bf),
            pltpu.VMEM((pairs, 2, 1, rows), f32),
            pltpu.VMEM((pairs, 2, 1, rows), f32),
            pltpu.VMEM((pairs, LANES, rows), f32),
            pltpu.VMEM((pairs, 2, 1, rows), f32),
            pltpu.VMEM((pairs, 2, 1, rows), f32),
            pltpu.VMEM((pairs, LANES, rows), f32),
            pltpu.VMEM((6, rows, rows), f32),
            pltpu.VMEM((pairs, LANES, rows), bf),
            pltpu.VMEM((pairs, LANES, rows), bf),
            pltpu.VMEM((pairs, 8, rows), f32),
            pltpu.VMEM((pairs, 8, rows), f32),
            pltpu.VMEM((8, LANES), f32),
            pltpu.VMEM((8, LANES), f32),
            pltpu.SemaphoreType.DMA((5,)),
            pltpu.SemaphoreType.DMA((2, 2)),
            pltpu.SemaphoreType.DMA((2, 2)),
            pltpu.SemaphoreType.DMA((pairs, 3)),
            pltpu.SemaphoreType.DMA((pairs, 3)),
            pltpu.SemaphoreType.DMA((2,)),
            pltpu.VMEM((rows, model), bf),
            pltpu.VMEM((rows, 3 * width), bf),
            pltpu.VMEM((rows, width), bf),
            pltpu.VMEM((heads, rows), f32),
            pltpu.VMEM((rows, heads), f32),
            pltpu.VMEM((rows, width), f32),
            pltpu.VMEM((64, width), f32),
            pltpu.VMEM((1, width), f32),
            pltpu.VMEM((64, width), f32),
            pltpu.VMEM((1, width), f32),
            pltpu.VMEM((rounds, 80, width), bf),
            pltpu.VMEM((rounds, 80, width), bf),
            pltpu.SemaphoreType.DMA((rounds,)),
            pltpu.SemaphoreType.DMA((rounds,)),
        ],
        compiler_params=pltpu.CompilerParams(
            collective_id=0, has_side_effects=True, vmem_limit_bytes=60 * 2**20
        ),
    )(
        frames, norm_gain1.reshape(1, model), w_qkv1, log_decay, head_gain.reshape(1, width),
        w_out1, norm_gain2.reshape(1, model), w_qkv2, window_ids,
    )
    parts = rows // LANES
    return pl.pallas_call(
        close_layer,
        out_shape=jax.ShapeDtypeStruct((rows, model), bf),
        in_specs=[vmem, vmem, vmem],
        out_specs=hbm,
        scratch_shapes=[
            pltpu.VMEM((rows, model), bf),
            pltpu.SemaphoreType.DMA((parts,)),
        ],
        compiler_params=pltpu.CompilerParams(vmem_limit_bytes=4 * 2**20),
    )(in_vmem(y), in_vmem(hid), in_vmem(w_out2))


def solution(mesh):
    placed = (
        P(("dp", "tm"), None),
        P(),
        P(),
        P(None, ("dp", "tm")),
        P(),
        P(),
        P(),
        P(),
        P(("dp", "tm"), None),
        P(),
    )
    return jax.shard_map(
        local, mesh=mesh, in_specs=placed, out_specs=P(("dp", "tm"), None), check_vma=False
    )
```

```python
import functools

import jax
import jax.numpy as jnp
from jax import lax
from jax.experimental import pallas as pl
from jax.experimental.pallas import tpu as pltpu
from jax.sharding import PartitionSpec as P

MESH = pl.DeviceIdType.MESH
TILE = 256
WIDE = 512
FAR = -1e30
LANES = 128
SCALE2 = 1.4426950408889634


def f32dot(a, b, dims=(((1,), (0,)), ((), ()))):
    return lax.dot_general(a, b, dims, preferred_element_type=jnp.float32)


def tile_at(index, size):
    return pl.ds(pl.multiple_of(index * size, size), size)


def norm_rows(src_ref, gain_ref, dst_ref):
    step = 256

    def body(i, carry):
        rows = tile_at(i, step)
        wide = src_ref[rows, :].astype(jnp.float32)
        scale = lax.rsqrt(jnp.mean(wide * wide, axis=-1, keepdims=True) + 1e-05)
        dst_ref[rows, :] = (wide * scale * gain_ref[...]).astype(jnp.bfloat16)
        return carry

    lax.fori_loop(0, src_ref.shape[0] // step, body, 0)


def both_layers(
    n,
    x_hbm, g1_hbm, w1_hbm, ld_hbm, hg_hbm, wo_hbm, g2_hbm, w2_hbm, ids_hbm,
    y_out, hid_ref,
    g1_ref, ld_ref, hg_ref, g2_ref, ids_ref, small_sem,
    x_ref, w1_ref, wo_ref, w2_ref, qt_ref, q_far, k_ref, v_ref,
    m_s, l_s, acc_s, s_s, o_send, o_recv, st_send, st_recv, bias_send, bias_recv,
    load_sem, kv_send, kv_recv, on_send, on_recv, far_send, far_recv, bias_sems,
    h_s, qkv_s, y_s, run_s, runt_s, lin_s, x_s, ax_s, e_s, em_s, a_s, send_b, recv_b, send_a, recv_a, send_sem, recv_sem,
):
    me = lax.axis_index("tm")
    small = [
        pltpu.make_async_copy(src, dst, small_sem.at[i])
        for i, (src, dst) in enumerate(
            [(ld_hbm, ld_ref), (g1_hbm, g1_ref), (hg_hbm, hg_ref), (g2_hbm, g2_ref), (ids_hbm, ids_ref)]
        )
    ]
    x_load = pltpu.make_async_copy(x_hbm, x_ref, load_sem.at[0])
    x_load.start()
    for load in small:
        load.start()
    rows = x_ref.shape[0]
    width = wo_ref.shape[0]
    heads = ld_ref.shape[0]
    pairs = width // LANES
    rounds = max(2, (n - 1).bit_length())
    dists = [1 << r for r in range(rounds)]

    barrier = pltpu.get_barrier_semaphore()
    for dist in dists:
        @pl.when(me + dist < n)
        def _():
            pl.semaphore_signal(barrier, inc=1, device_id={"tm": me + dist}, device_id_type=MESH)

        @pl.when(me >= dist)
        def _():
            pl.semaphore_signal(barrier, inc=1, device_id={"tm": me - dist}, device_id_type=MESH)

    loads = [
        pltpu.make_async_copy(src, dst, load_sem.at[i])
        for i, (src, dst) in enumerate(
            [
                (x_hbm, x_ref),
                (w1_hbm.at[:, width:], w1_ref.at[:, width:]),
                (w1_hbm.at[:, :width], w1_ref.at[:, :width]),
                (wo_hbm, wo_ref),
                (w2_hbm, w2_ref),
            ]
        )
    ]
    for load in loads[1:]:
        load.start()
    for load in small:
        load.wait()
    upper = (
        lax.broadcasted_iota(jnp.int32, (rows, rows), 0)
        <= lax.broadcasted_iota(jnp.int32, (rows, rows), 1)
    ).astype(jnp.float32)
    run = lax.dot_general(
        ld_ref[...], upper, (((1,), (0,)), ((), ())),
        precision=lax.Precision.HIGHEST, preferred_element_type=jnp.float32,
    )
    run_s[...] = run
    runt_s[...] = run.T
    last = run[:, rows - 1 : rows]
    headsel = lax.broadcasted_iota(jnp.int32, (heads, width), 1) // (
        width // heads
    ) == lax.broadcasted_iota(jnp.int32, (heads, width), 0)
    def by_lane(per_head):
        return jnp.sum(jnp.where(headsel, per_head[:, 0:1], 0.0), axis=0, keepdims=True)

    a_s[...] = jnp.broadcast_to(jnp.exp(last), a_s.shape)
    low = lax.broadcasted_iota(jnp.int32, (1, LANES), 1) < LANES // 2
    half = rows // 2
    mid = run[:, half - 1 : half]
    early = lax.broadcasted_iota(jnp.int32, (heads, rows), 1) < half
    left_t = jnp.exp(jnp.where(early, mid, last) - run).T
    runt_s[half:rows, :] = runt_s[half:rows, :] - runt_s[half - 1 : half, :]
    run_s[...] = jnp.where(early, run, run - mid)
    mid_row, rest_row = by_lane(jnp.exp(mid)), by_lane(jnp.exp(last - mid))

    loads[0].wait()
    norm_rows(x_ref, g1_ref, h_s)
    loads[1].wait()

    def project(j, carry):
        cols = tile_at(j, WIDE)
        qkv_s[:, cols] = f32dot(h_s[...], w1_ref[:, cols]).astype(jnp.bfloat16)
        return carry

    lax.fori_loop(width // WIDE, 3 * width // WIDE, project, 0)

    for p in range(pairs):
        cols = slice(p * LANES, (p + 1) * LANES)
        kcols = slice(width + p * LANES, width + (p + 1) * LANES)
        vcols = slice(2 * width + p * LANES, 2 * width + (p + 1) * LANES)
        decay = jnp.where(low, left_t[:, 2 * p : 2 * p + 1], left_t[:, 2 * p + 1 : 2 * p + 2])
        keyed = (qkv_s[:, kcols].astype(jnp.float32) * decay).astype(jnp.bfloat16).T
        ends = []
        for first in (0, half):
            full = f32dot(keyed[:, first : first + half], qkv_s[first : first + half, vcols])
            ends.append(jnp.where(low, full[: LANES // 2], full[LANES // 2 :]))
        em_s[:, cols] = ends[0]
        e_s[:, cols] = ends[0] * rest_row[:, cols] + ends[1]
    x_s[...] = jnp.zeros_like(x_s)
    ax_s[...] = jnp.ones_like(ax_s)

    def send(r, dist):
        @pl.when(me + dist < n)
        def _():
            send_b[r] = (e_s[...] + by_lane(a_s[...]) * x_s[...]).astype(jnp.bfloat16)
            send_a[r] = a_s[...] * ax_s[...]
            for copy in copy_of(r, dist):
                copy.start()

    def copy_of(r, dist):
        return [
            pltpu.make_async_remote_copy(
                src_ref=src.at[r], dst_ref=dst.at[r],
                send_sem=send_sem.at[r, i], recv_sem=recv_sem.at[r, i],
                device_id={"tm": me + dist}, device_id_type=MESH,
            )
            for i, (src, dst) in enumerate([(send_b, recv_b), (send_a, recv_a)])
        ]

    def receive(r, dist):
        @pl.when(me >= dist)
        def _():
            for copy in copy_of(r, dist):
                copy.wait_recv()
            x_s[...] = x_s[...] + by_lane(ax_s[...]) * recv_b[r].astype(jnp.float32)
            ax_s[...] = ax_s[...] * recv_a[r]

    peers = [me + dist < n for dist in dists] + [me >= dist for dist in dists]
    pl.semaphore_wait(barrier, sum(peer.astype(jnp.int32) for peer in peers))

    core = lax.rem(me, 2)
    even = core == 0
    odd = jnp.logical_not(even)
    helps = me + 2 < n
    helped = me >= 2
    hands_on = jnp.logical_and(odd, me + 3 < n)
    gets_prev = jnp.logical_and(even, jnp.logical_and(me >= 2, helps))

    def listing(back):
        listed = ids_ref[0, 0] == me - back
        for j in range(1, ids_ref.shape[1]):
            listed = jnp.logical_or(listed, ids_ref[0, j] == me - back)
        return jnp.where(listed, jnp.float32(0.0), jnp.float32(FAR))

    def bias_back():
        return pltpu.make_async_remote_copy(
            src_ref=bias_send, dst_ref=bias_recv,
            send_sem=bias_sems.at[0], recv_sem=bias_sems.at[1],
            device_id={"tm": me - 2}, device_id_type=MESH,
        )

    near = jnp.where(even, listing(1), listing(3))
    brow = lax.broadcasted_iota(jnp.int32, bias_send.shape, 0)
    bias_send[...] = jnp.where(brow == 0, listing(2), jnp.where(brow == 1, near, listing(3)))

    @pl.when(helped)
    def _():
        bias_back().start()

    def work_query():
        loads[2].wait()
        lax.fori_loop(0, width // WIDE, project, 0)

    def work_pair(p):
        cols = slice(p * LANES, (p + 1) * LANES)
        kcols = slice(width + p * LANES, width + (p + 1) * LANES)
        vcols = slice(2 * width + p * LANES, 2 * width + (p + 1) * LANES)
        causal = lax.broadcasted_iota(jnp.int32, (half, half), 0) >= (
            lax.broadcasted_iota(jnp.int32, (half, half), 1)
        )
        for first in range(0, rows, half):
            upto = first + half
            parts = []
            query = qkv_s[first:upto, cols]
            keys = qkv_s[first:upto, kcols]
            vals = qkv_s[first:upto, vcols]
            for side in range(2):
                h = 2 * p + side
                keep = low if side == 0 else jnp.logical_not(low)
                mine = jnp.where(keep, query.astype(jnp.float32), 0.0).astype(jnp.bfloat16)
                scores = f32dot(mine, keys, (((1,), (1,)), ((), ())))
                diff = runt_s[first:upto, h : h + 1] - run_s[h : h + 1, first:upto]
                weight = jnp.where(causal, jnp.exp(jnp.minimum(diff, 0.0)), 0.0)
                parts.append(f32dot((scores * weight).astype(jnp.bfloat16), vals))
            lin_s[first:upto, cols] = jnp.where(low, parts[0], parts[1])

    work = [work_query] + [functools.partial(work_pair, p) for p in range(pairs)]
    def send_after(r):
        if r < rounds:
            @pl.when(me >= (dists[r - 1] if r else 0))
            def _():
                send(r, dists[r])

        if r + 1 < rounds:
            @pl.when(jnp.logical_and(me >= (dists[r - 1] if r else 0), me < dists[r]))
            def _():
                for later in range(r + 1, rounds):
                    send(later, dists[later])

    send_after(0)
    for r, dist in enumerate(dists):
        take = 1 if r < rounds - 1 else len(work)
        if r == 1:
            take = 2
        for item in work[:take]:
            item()
        work = work[take:]
        receive(r, dist)
        send_after(r + 1)
    for item in work:
        item()

    side_of = [lax.broadcasted_iota(jnp.int32, (LANES, LANES), d) // 64 for d in (0, 1)]
    same_head = (side_of[0] == side_of[1]).astype(jnp.float32).astype(jnp.bfloat16)
    for p in range(pairs):
        cols = slice(p * LANES, (p + 1) * LANES)
        grow = jnp.exp(
            jnp.where(low, runt_s[:, 2 * p : 2 * p + 1], runt_s[:, 2 * p + 1 : 2 * p + 2])
        )
        scaled = (qkv_s[:, cols].astype(jnp.float32) * grow).astype(jnp.bfloat16)
        before = x_s[:, cols]
        inter = []
        for first, packed in ((0, before), (half, before * mid_row[:, cols] + em_s[:, cols])):
            state = jnp.concatenate(
                [jnp.where(low, packed, 0.0), jnp.where(low, 0.0, packed)], axis=0
            ).astype(jnp.bfloat16)
            inter.append(f32dot(scaled[first : first + half], state))
        lin = lin_s[:, cols] + jnp.concatenate(inter, axis=0)
        square = lin * lin
        high = square.astype(jnp.bfloat16)
        rest = (square - high.astype(jnp.float32)).astype(jnp.bfloat16)
        mean = (f32dot(high, same_head) + f32dot(rest, same_head)) * (1.0 / 64)
        y_s[:, cols] = (lin * lax.rsqrt(mean + 1e-06) * hg_ref[:, cols]).astype(jnp.bfloat16)

    def out_tile(j, carry):
        cols = tile_at(j, WIDE)
        branch = f32dot(y_s[...], wo_ref[:, cols])
        hid_ref[:, cols] = (x_ref[:, cols].astype(jnp.float32) + branch).astype(jnp.bfloat16)
        return carry

    loads[3].wait()
    lax.fori_loop(0, x_ref.shape[1] // WIDE, out_tile, 0)
    loads[4].wait()
    norm_rows(hid_ref, g2_ref, h_s)

    def query_back(p):
        return pltpu.make_async_remote_copy(
            src_ref=qt_ref.at[p], dst_ref=q_far.at[p],
            send_sem=far_send.at[p, 0], recv_sem=far_recv.at[p, 0],
            device_id={"tm": me - 2}, device_id_type=MESH,
        )

    def partial_on(p):
        return [
            pltpu.make_async_remote_copy(
                src_ref=src.at[p], dst_ref=dst.at[p],
                send_sem=far_send.at[p, i], recv_sem=far_recv.at[p, i],
                device_id={"tm": me + 2}, device_id_type=MESH,
            )
            for i, (src, dst) in [(1, (o_send, o_recv)), (2, (st_send, st_recv))]
        ]

    sib = [
        pltpu.make_async_remote_copy(
            src_ref=ref.at[0], dst_ref=ref.at[1],
            send_sem=kv_send.at[i], recv_sem=kv_recv.at[i],
            device_id={"tm": me + 1 - 2 * core}, device_id_type=MESH,
        )
        for i, ref in enumerate([k_ref, v_ref])
    ]

    def keys_on():
        return pltpu.make_async_remote_copy(
            src_ref=k_ref.at[0], dst_ref=k_ref.at[2],
            send_sem=on_send.at[pairs], recv_sem=on_recv.at[pairs],
            device_id={"tm": me + 1}, device_id_type=MESH,
        )

    def values_on(p):
        return pltpu.make_async_remote_copy(
            src_ref=v_ref.at[0, p], dst_ref=v_ref.at[2, p],
            send_sem=on_send.at[p], recv_sem=on_recv.at[p],
            device_id={"tm": me + 1}, device_id_type=MESH,
        )

    def queries():
        block = f32dot(h_s[...], w2_ref[:, 0:width]) * (SCALE2 * 64 ** (-0.5))
        for p in range(pairs):
            qt_ref[p] = block[:, p * LANES : (p + 1) * LANES].astype(jnp.bfloat16).T

            @pl.when(helped)
            def _():
                query_back(p).start()

    def keys():
        block = f32dot(h_s[...], w2_ref[:, width : 2 * width]).astype(jnp.bfloat16)
        for p in range(pairs):
            k_ref[0, p] = block[:, p * LANES : (p + 1) * LANES]

    def values():
        block = f32dot(h_s[...], w2_ref[:, 2 * width : 3 * width])
        for p in range(pairs):
            v_ref[0, p] = block[:, p * LANES : (p + 1) * LANES].astype(jnp.bfloat16).T

    @pl.when(jnp.logical_not(hands_on))
    def _():
        queries()
        keys()
        sib[0].start()
        values()
        sib[1].start()

    @pl.when(hands_on)
    def _():
        keys()
        keys_on().start()
        sib[0].start()
        values()
        for p in range(pairs):
            values_on(p).start()

        sib[1].start()
        queries()

    half_rows = LANES // 2
    blank = jnp.zeros((half_rows, rows), jnp.bfloat16)

    def pair_attend(p, query, slots, biases, put):
        def score(side):
            own = query[side * half_rows : (side + 1) * half_rows, :]
            mine = jnp.concatenate([own, blank] if side == 0 else [blank, own], axis=0)
            tops = []
            for j, slot in enumerate(slots):
                s = f32dot(k_ref[slot, p], mine)
                s_s[side * 3 + j] = s
                tops.append(jnp.max(s, axis=0, keepdims=True))
            best = functools.reduce(
                jnp.maximum, [top + bias for top, bias in zip(tops, biases)]
            )
            return best, [jnp.maximum(best - bias, top) for top, bias in zip(tops, biases)]

        def soft(side, best, refs):
            total, acc = None, None
            for j, slot in enumerate(slots):
                w = jnp.exp2(s_s[side * 3 + j] - refs[j])
                add = jnp.sum(w, axis=0, keepdims=True)
                part = f32dot(
                    v_ref[slot, p, side * half_rows : (side + 1) * half_rows, :],
                    w.astype(jnp.bfloat16),
                )
                total = add if total is None else total + add
                acc = part if acc is None else acc + part
            put(p, side, best, total, acc)

        first = score(0)
        second = score(1)
        soft(0, *first)
        soft(1, *second)

    def put_merged(p, side, best, total, acc):
        arow = slice(side * half_rows, (side + 1) * half_rows)
        m_old = m_s[p, side]
        m_new = jnp.maximum(m_old, best)
        alpha, beta = jnp.exp2(m_old - m_new), jnp.exp2(best - m_new)
        m_s[p, side] = m_new
        l_s[p, side] = l_s[p, side] * alpha + total * beta
        acc_s[p, arow, :] = acc_s[p, arow, :] * alpha + acc * beta

    def put_far(p, side, best, total, acc):
        st_send[p, side : side + 1, :] = best
        st_send[p, side + 2 : side + 3, :] = total
        o_send[p, side * half_rows : (side + 1) * half_rows, :] = acc.astype(jnp.bfloat16)

    def loop_pairs(body):
        def step(p, carry):
            body(p)
            return carry

        lax.fori_loop(0, pairs, step, 0)

    own_mask = lax.broadcasted_iota(jnp.int32, (half, half), 0) <= (
        lax.broadcasted_iota(jnp.int32, (half, half), 1)
    )

    def own_attend(p):
        query = qt_ref[p]

        def score(side):
            own = query[side * half_rows : (side + 1) * half_rows, :]
            mine = jnp.concatenate([own, blank] if side == 0 else [blank, own], axis=0)
            s = f32dot(k_ref[0, p, 0:half, :], mine)
            left, right = jnp.where(own_mask, s[:, 0:half], FAR), s[:, half:rows]
            low_right = f32dot(k_ref[0, p, half:rows, :], mine[:, half:rows])
            low_right = jnp.where(own_mask, low_right, FAR)
            s_s[side, 0:half, 0:half] = left
            s_s[side, 0:half, half:rows] = right
            s_s[side, half:rows, half:rows] = low_right
            top = jnp.maximum(
                jnp.max(right, axis=0, keepdims=True), jnp.max(low_right, axis=0, keepdims=True)
            )
            return jnp.concatenate([jnp.max(left, axis=0, keepdims=True), top], axis=1)

        def soft(side, best):
            arow = slice(side * half_rows, (side + 1) * half_rows)
            w = jnp.exp2(s_s[side, 0:half, :] - best)
            late = jnp.exp2(s_s[side, half:rows, half:rows] - best[:, half:rows])
            total = jnp.sum(w, axis=0, keepdims=True)
            part = f32dot(v_ref[0, p, arow, 0:half], w.astype(jnp.bfloat16))
            more = f32dot(v_ref[0, p, arow, half:rows], late.astype(jnp.bfloat16))
            m_s[p, side] = best
            l_s[p, side, :, 0:half] = total[:, 0:half]
            l_s[p, side, :, half:rows] = total[:, half:rows] + jnp.sum(late, axis=0, keepdims=True)
            acc_s[p, arow, 0:half] = part[:, 0:half]
            acc_s[p, arow, half:rows] = part[:, half:rows] + more

        tops = [score(side) for side in range(2)]
        for side in range(2):
            soft(side, tops[side])

    loop_pairs(own_attend)
    for copy in sib:
        copy.wait_recv()

    def help_bias(j):
        return bias_recv[j : j + 1, 0:1]

    def give(p):
        for copy in partial_on(p):
            copy.start()

    def near_part(p, put):
        query_back(p).wait_recv()
        pair_attend(p, q_far[p], [0, 1], [help_bias(0), help_bias(1)], put)

    @pl.when(helps)
    def _():
        bias_back().wait_recv()

    @pl.when(gets_prev)
    def _():
        keys_on().wait_recv()
        biases = [help_bias(j) for j in range(3)]

        def body(p):
            query_back(p).wait_recv()
            values_on(p).wait_recv()
            pair_attend(p, q_far[p], [0, 1, 2], biases, put_far)
            give(p)

        loop_pairs(body)

    @pl.when(jnp.logical_and(even, jnp.logical_and(helps, jnp.logical_not(gets_prev))))
    def _():
        def body(p):
            near_part(p, put_far)
            give(p)

        loop_pairs(body)

    @pl.when(odd)
    def _():
        bias = listing(1)

        @pl.when(helps)
        def _():
            def body(p):
                near_part(p, put_far)
                give(p)

            loop_pairs(body)

        loop_pairs(lambda p: pair_attend(p, qt_ref[p], [1], [bias], put_merged))

    for p in range(pairs):
        @pl.when(helped)
        def _():
            for copy in partial_on(p):
                copy.wait_recv()
            for half in range(2):
                far = o_recv[p, half * half_rows : (half + 1) * half_rows, :]
                put_merged(
                    p, half, st_recv[p, half : half + 1, :],
                    st_recv[p, half + 2 : half + 3, :], far.astype(jnp.float32),
                )

        whole = jnp.concatenate(
            [
                acc_s[p, 0:half_rows, :] * (1.0 / l_s[p, 0]),
                acc_s[p, half_rows:LANES, :] * (1.0 / l_s[p, 1]),
            ],
            axis=0,
        )
        y_out[:, p * LANES : (p + 1) * LANES] = whole.T.astype(jnp.bfloat16)

    def drain(copies):
        for copy in copies:
            copy.wait_send()

    for r, dist in enumerate(dists):
        @pl.when(me + dist < n)
        def _():
            for copy in copy_of(r, dist):
                copy.wait_send()

    drain(sib)

    @pl.when(hands_on)
    def _():
        drain([keys_on()] + [values_on(p) for p in range(pairs)])

    @pl.when(helped)
    def _():
        drain([bias_back()])

    for p in range(pairs):
        @pl.when(helped)
        def _():
            drain([query_back(p)])

        @pl.when(helps)
        def _():
            drain(partial_on(p))


def close_layer(y_ref, hid_ref, wp_ref, out_hbm, out_ref, sems):
    copies = []
    for i in range(out_ref.shape[0] // LANES):
        rows = slice(i * LANES, (i + 1) * LANES)
        branch = f32dot(y_ref[rows, :], wp_ref[...])
        out_ref[rows, :] = (hid_ref[rows, :].astype(jnp.float32) + branch).astype(jnp.bfloat16)
        copies.append(pltpu.make_async_copy(out_ref.at[rows], out_hbm.at[rows], sems.at[i]))
        copies[-1].start()
    for copy in copies:
        copy.wait()


def in_vmem(array):
    return pltpu.with_memory_space_constraint(array, pltpu.VMEM)


def local(
    frames, norm_gain1, w_qkv1, log_decay, head_gain, w_out1, norm_gain2, w_qkv2, window_ids, w_out2
):
    n = lax.axis_size("tm")
    rows, model = frames.shape
    width = w_out1.shape[0]
    heads = log_decay.shape[0]
    rounds = max(2, (n - 1).bit_length())
    pairs = width // LANES
    vmem = pl.BlockSpec(memory_space=pltpu.VMEM)
    hbm = pl.BlockSpec(memory_space=pltpu.HBM)
    bf, f32 = jnp.bfloat16, jnp.float32
    y, hid = pl.pallas_call(
        functools.partial(both_layers, n),
        out_shape=[
            pltpu.VMEM((rows, width), bf),
            pltpu.VMEM((rows, model), bf),
        ],
        in_specs=[hbm] * 9,
        out_specs=[vmem, vmem],
        scratch_shapes=[
            pltpu.VMEM((1, model), f32),
            pltpu.VMEM((heads, rows), f32),
            pltpu.VMEM((1, width), f32),
            pltpu.VMEM((1, model), f32),
            pltpu.SMEM(window_ids.shape, jnp.int32),
            pltpu.SemaphoreType.DMA((5,)),
            pltpu.VMEM((rows, model), bf),
            pltpu.VMEM((model, 3 * width), bf),
            pltpu.VMEM((width, model), bf),
            pltpu.VMEM((model, 3 * width), bf),
            pltpu.VMEM((pairs, LANES, rows), bf),
            pltpu.VMEM((pairs, LANES, rows), bf),
            pltpu.VMEM((3, pairs, rows, LANES), bf),
            pltpu.VMEM((3, pairs, LANES, rows), bf),
            pltpu.VMEM((pairs, 2, 1, rows), f32),
            pltpu.VMEM((pairs, 2, 1, rows), f32),
            pltpu.VMEM((pairs, LANES, rows), f32),
            pltpu.VMEM((6, rows, rows), f32),
            pltpu.VMEM((pairs, LANES, rows), bf),
            pltpu.VMEM((pairs, LANES, rows), bf),
            pltpu.VMEM((pairs, 4, rows), f32),
            pltpu.VMEM((pairs, 4, rows), f32),
            pltpu.VMEM((8, LANES), f32),
            pltpu.VMEM((8, LANES), f32),
            pltpu.SemaphoreType.DMA((5,)),
            pltpu.SemaphoreType.DMA((2,)),
            pltpu.SemaphoreType.DMA((2,)),
            pltpu.SemaphoreType.DMA((pairs + 1,)),
            pltpu.SemaphoreType.DMA((pairs + 1,)),
            pltpu.SemaphoreType.DMA((pairs, 3)),
            pltpu.SemaphoreType.DMA((pairs, 3)),
            pltpu.SemaphoreType.DMA((2,)),
            pltpu.VMEM((rows, model), bf),
            pltpu.VMEM((rows, 3 * width), bf),
            pltpu.VMEM((rows, width), bf),
            pltpu.VMEM((heads, rows), f32),
            pltpu.VMEM((rows, heads), f32),
            pltpu.VMEM((rows, width), f32),
            pltpu.VMEM((64, width), f32),
            pltpu.VMEM((heads, LANES), f32),
            pltpu.VMEM((64, width), f32),
            pltpu.VMEM((64, width), f32),
            pltpu.VMEM((heads, LANES), f32),
            pltpu.VMEM((rounds, 64, width), bf),
            pltpu.VMEM((rounds, 64, width), bf),
            pltpu.VMEM((rounds, heads, LANES), f32),
            pltpu.VMEM((rounds, heads, LANES), f32),
            pltpu.SemaphoreType.DMA((rounds, 2)),
            pltpu.SemaphoreType.DMA((rounds, 2)),
        ],
        compiler_params=pltpu.CompilerParams(
            collective_id=0, has_side_effects=True, vmem_limit_bytes=60 * 2**20
        ),
    )(
        frames, norm_gain1.reshape(1, model), w_qkv1, log_decay, head_gain.reshape(1, width),
        w_out1, norm_gain2.reshape(1, model), w_qkv2, window_ids,
    )
    parts = rows // LANES
    return pl.pallas_call(
        close_layer,
        out_shape=jax.ShapeDtypeStruct((rows, model), bf),
        in_specs=[vmem, vmem, vmem],
        out_specs=hbm,
        scratch_shapes=[
            pltpu.VMEM((rows, model), bf),
            pltpu.SemaphoreType.DMA((parts,)),
        ],
        compiler_params=pltpu.CompilerParams(vmem_limit_bytes=4 * 2**20),
    )(in_vmem(y), in_vmem(hid), in_vmem(w_out2))


def solution(mesh):
    placed = (
        P(("dp", "tm"), None),
        P(),
        P(),
        P(None, ("dp", "tm")),
        P(),
        P(),
        P(),
        P(),
        P(("dp", "tm"), None),
        P(),
    )
    return jax.shard_map(
        local, mesh=mesh, in_specs=placed, out_specs=P(("dp", "tm"), None), check_vma=False
    )
```

```python
import functools

import jax
import jax.numpy as jnp
from jax import lax
from jax.experimental import pallas as pl
from jax.experimental.pallas import tpu as pltpu
from jax.sharding import PartitionSpec as P

MESH = pl.DeviceIdType.MESH
TILE = 256
WIDE = 512
FAR = -1e30
LANES = 128
SCALE2 = 1.4426950408889634


def f32dot(a, b, dims=(((1,), (0,)), ((), ()))):
    return lax.dot_general(a, b, dims, preferred_element_type=jnp.float32)


def tile_at(index, size):
    return pl.ds(pl.multiple_of(index * size, size), size)


def norm_rows(src_ref, gain_ref, dst_ref):
    step = 256

    def body(i, carry):
        rows = tile_at(i, step)
        wide = src_ref[rows, :].astype(jnp.float32)
        scale = lax.rsqrt(jnp.mean(wide * wide, axis=-1, keepdims=True) + 1e-05)
        dst_ref[rows, :] = (wide * scale * gain_ref[...]).astype(jnp.bfloat16)
        return carry

    lax.fori_loop(0, src_ref.shape[0] // step, body, 0)


def both_layers(
    n,
    x_hbm, g1_hbm, w1_hbm, ld_hbm, hg_hbm, wo_hbm, g2_hbm, w2_hbm, ids_hbm, wp_hbm,
    y_last, sum_ref,
    g1_ref, ld_ref, hg_ref, g2_ref, ids_ref, small_sem,
    wp_ref, hid_ref,
    x_ref, w1_ref, wo_ref, w2_ref, qt_ref, q_far, k_ref, v_ref,
    m_s, l_s, acc_s, s_s, o_send, o_recv, st_send, st_recv, bias_send, bias_recv,
    load_sem, kv_send, kv_recv, on_send, on_recv, far_send, far_recv, bias_sems,
    h_s, qkv_s, y_s, run_s, runt_s, lin_s, x_s, ax_s, e_s, em_s, a_s, send_b, recv_b, send_a, recv_a, send_sem, recv_sem,
):
    me = lax.axis_index("tm")
    small = [
        pltpu.make_async_copy(src, dst, small_sem.at[i])
        for i, (src, dst) in enumerate(
            [(ld_hbm, ld_ref), (g1_hbm, g1_ref), (hg_hbm, hg_ref), (g2_hbm, g2_ref), (ids_hbm, ids_ref)]
        )
    ]
    x_load = pltpu.make_async_copy(x_hbm, x_ref, load_sem.at[0])
    x_load.start()
    for load in small:
        load.start()
    rows = x_ref.shape[0]
    width = wo_ref.shape[0]
    heads = ld_ref.shape[0]
    pairs = width // LANES
    rounds = max(2, (n - 1).bit_length())
    dists = [1 << r for r in range(rounds)]

    barrier = pltpu.get_barrier_semaphore()
    for dist in dists:
        @pl.when(me + dist < n)
        def _():
            pl.semaphore_signal(barrier, inc=1, device_id={"tm": me + dist}, device_id_type=MESH)

        @pl.when(me >= dist)
        def _():
            pl.semaphore_signal(barrier, inc=1, device_id={"tm": me - dist}, device_id_type=MESH)

    loads = [
        pltpu.make_async_copy(src, dst, load_sem.at[i])
        for i, (src, dst) in enumerate(
            [
                (x_hbm, x_ref),
                (w1_hbm.at[:, width:], w1_ref.at[:, width:]),
                (w1_hbm.at[:, :width], w1_ref.at[:, :width]),
                (wo_hbm, wo_ref),
                (w2_hbm, w2_ref),
                (wp_hbm, wp_ref),
            ]
        )
    ]
    for load in loads[1:]:
        load.start()
    for load in small:
        load.wait()
    upper = (
        lax.broadcasted_iota(jnp.int32, (rows, rows), 0)
        <= lax.broadcasted_iota(jnp.int32, (rows, rows), 1)
    ).astype(jnp.float32)
    run = lax.dot_general(
        ld_ref[...], upper, (((1,), (0,)), ((), ())),
        precision=lax.Precision.HIGHEST, preferred_element_type=jnp.float32,
    )
    run_s[...] = run
    runt_s[...] = run.T
    last = run[:, rows - 1 : rows]
    headsel = lax.broadcasted_iota(jnp.int32, (heads, width), 1) // (
        width // heads
    ) == lax.broadcasted_iota(jnp.int32, (heads, width), 0)
    def by_lane(per_head):
        return jnp.sum(jnp.where(headsel, per_head[:, 0:1], 0.0), axis=0, keepdims=True)

    a_s[...] = jnp.broadcast_to(jnp.exp(last), a_s.shape)
    low = lax.broadcasted_iota(jnp.int32, (1, LANES), 1) < LANES // 2
    half = rows // 2
    mid = run[:, half - 1 : half]
    early = lax.broadcasted_iota(jnp.int32, (heads, rows), 1) < half
    left_t = jnp.exp(jnp.where(early, mid, last) - run).T
    runt_s[half:rows, :] = runt_s[half:rows, :] - runt_s[half - 1 : half, :]
    run_s[...] = jnp.where(early, run, run - mid)
    mid_row, rest_row = by_lane(jnp.exp(mid)), by_lane(jnp.exp(last - mid))

    loads[0].wait()
    norm_rows(x_ref, g1_ref, h_s)
    loads[1].wait()

    def project(j, carry):
        cols = tile_at(j, WIDE)
        qkv_s[:, cols] = f32dot(h_s[...], w1_ref[:, cols]).astype(jnp.bfloat16)
        return carry

    lax.fori_loop(width // WIDE, 3 * width // WIDE, project, 0)

    for p in range(pairs):
        cols = slice(p * LANES, (p + 1) * LANES)
        kcols = slice(width + p * LANES, width + (p + 1) * LANES)
        vcols = slice(2 * width + p * LANES, 2 * width + (p + 1) * LANES)
        decay = jnp.where(low, left_t[:, 2 * p : 2 * p + 1], left_t[:, 2 * p + 1 : 2 * p + 2])
        keyed = (qkv_s[:, kcols].astype(jnp.float32) * decay).astype(jnp.bfloat16).T
        ends = []
        for first in (0, half):
            full = f32dot(keyed[:, first : first + half], qkv_s[first : first + half, vcols])
            ends.append(jnp.where(low, full[: LANES // 2], full[LANES // 2 :]))
        em_s[:, cols] = ends[0]
        e_s[:, cols] = ends[0] * rest_row[:, cols] + ends[1]
    x_s[...] = jnp.zeros_like(x_s)
    ax_s[...] = jnp.ones_like(ax_s)

    def send(r, dist):
        @pl.when(me + dist < n)
        def _():
            send_b[r] = (e_s[...] + by_lane(a_s[...]) * x_s[...]).astype(jnp.bfloat16)
            send_a[r] = a_s[...] * ax_s[...]
            for copy in copy_of(r, dist):
                copy.start()

    def copy_of(r, dist):
        return [
            pltpu.make_async_remote_copy(
                src_ref=src.at[r], dst_ref=dst.at[r],
                send_sem=send_sem.at[r, i], recv_sem=recv_sem.at[r, i],
                device_id={"tm": me + dist}, device_id_type=MESH,
            )
            for i, (src, dst) in enumerate([(send_b, recv_b), (send_a, recv_a)])
        ]

    def receive(r, dist):
        @pl.when(me >= dist)
        def _():
            for copy in copy_of(r, dist):
                copy.wait_recv()
            x_s[...] = x_s[...] + by_lane(ax_s[...]) * recv_b[r].astype(jnp.float32)
            ax_s[...] = ax_s[...] * recv_a[r]

    peers = [me + dist < n for dist in dists] + [me >= dist for dist in dists]
    pl.semaphore_wait(barrier, sum(peer.astype(jnp.int32) for peer in peers))

    core = lax.rem(me, 2)
    even = core == 0
    odd = jnp.logical_not(even)
    helps = me + 2 < n
    helped = me >= 2
    hands_on = jnp.logical_and(odd, me + 3 < n)
    gets_prev = jnp.logical_and(even, jnp.logical_and(me >= 2, helps))

    def listing(back):
        listed = ids_ref[0, 0] == me - back
        for j in range(1, ids_ref.shape[1]):
            listed = jnp.logical_or(listed, ids_ref[0, j] == me - back)
        return jnp.where(listed, jnp.float32(0.0), jnp.float32(FAR))

    def bias_back():
        return pltpu.make_async_remote_copy(
            src_ref=bias_send, dst_ref=bias_recv,
            send_sem=bias_sems.at[0], recv_sem=bias_sems.at[1],
            device_id={"tm": me - 2}, device_id_type=MESH,
        )

    near = jnp.where(even, listing(1), listing(3))
    brow = lax.broadcasted_iota(jnp.int32, bias_send.shape, 0)
    bias_send[...] = jnp.where(brow == 0, listing(2), jnp.where(brow == 1, near, listing(3)))

    @pl.when(helped)
    def _():
        bias_back().start()

    def work_query():
        loads[2].wait()
        lax.fori_loop(0, width // WIDE, project, 0)

    def work_pair(p):
        cols = slice(p * LANES, (p + 1) * LANES)
        kcols = slice(width + p * LANES, width + (p + 1) * LANES)
        vcols = slice(2 * width + p * LANES, 2 * width + (p + 1) * LANES)
        causal = lax.broadcasted_iota(jnp.int32, (half, half), 0) >= (
            lax.broadcasted_iota(jnp.int32, (half, half), 1)
        )
        for first in range(0, rows, half):
            upto = first + half
            parts = []
            query = qkv_s[first:upto, cols]
            keys = qkv_s[first:upto, kcols]
            vals = qkv_s[first:upto, vcols]
            for side in range(2):
                h = 2 * p + side
                keep = low if side == 0 else jnp.logical_not(low)
                mine = jnp.where(keep, query.astype(jnp.float32), 0.0).astype(jnp.bfloat16)
                scores = f32dot(mine, keys, (((1,), (1,)), ((), ())))
                diff = runt_s[first:upto, h : h + 1] - run_s[h : h + 1, first:upto]
                weight = jnp.where(causal, jnp.exp(jnp.minimum(diff, 0.0)), 0.0)
                parts.append(f32dot((scores * weight).astype(jnp.bfloat16), vals))
            lin_s[first:upto, cols] = jnp.where(low, parts[0], parts[1])

    work = [work_query] + [functools.partial(work_pair, p) for p in range(pairs)]
    def send_after(r):
        if r < rounds:
            @pl.when(me >= (dists[r - 1] if r else 0))
            def _():
                send(r, dists[r])

        if r + 1 < rounds:
            @pl.when(jnp.logical_and(me >= (dists[r - 1] if r else 0), me < dists[r]))
            def _():
                for later in range(r + 1, rounds):
                    send(later, dists[later])

    send_after(0)
    for r, dist in enumerate(dists):
        take = 1 if r == 0 else len(work)
        for item in work[:take]:
            item()
        work = work[take:]
        receive(r, dist)
        send_after(r + 1)
    for item in work:
        item()

    side_of = [lax.broadcasted_iota(jnp.int32, (LANES, LANES), d) // 64 for d in (0, 1)]
    same_head = (side_of[0] == side_of[1]).astype(jnp.float32).astype(jnp.bfloat16)
    for p in range(pairs):
        cols = slice(p * LANES, (p + 1) * LANES)
        grow = jnp.exp(
            jnp.where(low, runt_s[:, 2 * p : 2 * p + 1], runt_s[:, 2 * p + 1 : 2 * p + 2])
        )
        scaled = (qkv_s[:, cols].astype(jnp.float32) * grow).astype(jnp.bfloat16)
        before = x_s[:, cols]
        inter = []
        for first, packed in ((0, before), (half, before * mid_row[:, cols] + em_s[:, cols])):
            state = jnp.concatenate(
                [jnp.where(low, packed, 0.0), jnp.where(low, 0.0, packed)], axis=0
            ).astype(jnp.bfloat16)
            inter.append(f32dot(scaled[first : first + half], state))
        lin = lin_s[:, cols] + jnp.concatenate(inter, axis=0)
        square = lin * lin
        high = square.astype(jnp.bfloat16)
        rest = (square - high.astype(jnp.float32)).astype(jnp.bfloat16)
        mean = (f32dot(high, same_head) + f32dot(rest, same_head)) * (1.0 / 64)
        y_s[:, cols] = (lin * lax.rsqrt(mean + 1e-06) * hg_ref[:, cols]).astype(jnp.bfloat16)

    def out_tile(j, carry):
        cols = tile_at(j, WIDE)
        branch = f32dot(y_s[...], wo_ref[:, cols])
        hid_ref[:, cols] = (x_ref[:, cols].astype(jnp.float32) + branch).astype(jnp.bfloat16)
        return carry

    loads[3].wait()
    lax.fori_loop(0, x_ref.shape[1] // WIDE, out_tile, 0)
    loads[4].wait()
    norm_rows(hid_ref, g2_ref, h_s)

    def query_back(p):
        return pltpu.make_async_remote_copy(
            src_ref=qt_ref.at[p], dst_ref=q_far.at[p],
            send_sem=far_send.at[p, 0], recv_sem=far_recv.at[p, 0],
            device_id={"tm": me - 2}, device_id_type=MESH,
        )

    def partial_on(p):
        return [
            pltpu.make_async_remote_copy(
                src_ref=src.at[p], dst_ref=dst.at[p],
                send_sem=far_send.at[p, i], recv_sem=far_recv.at[p, i],
                device_id={"tm": me + 2}, device_id_type=MESH,
            )
            for i, (src, dst) in [(1, (o_send, o_recv)), (2, (st_send, st_recv))]
        ]

    sib = [
        pltpu.make_async_remote_copy(
            src_ref=ref.at[0], dst_ref=ref.at[1],
            send_sem=kv_send.at[i], recv_sem=kv_recv.at[i],
            device_id={"tm": me + 1 - 2 * core}, device_id_type=MESH,
        )
        for i, ref in enumerate([k_ref, v_ref])
    ]

    def keys_on():
        return pltpu.make_async_remote_copy(
            src_ref=k_ref.at[0], dst_ref=k_ref.at[2],
            send_sem=on_send.at[pairs], recv_sem=on_recv.at[pairs],
            device_id={"tm": me + 1}, device_id_type=MESH,
        )

    def values_on(p):
        return pltpu.make_async_remote_copy(
            src_ref=v_ref.at[0, p], dst_ref=v_ref.at[2, p],
            send_sem=on_send.at[p], recv_sem=on_recv.at[p],
            device_id={"tm": me + 1}, device_id_type=MESH,
        )

    def queries():
        block = f32dot(h_s[...], w2_ref[:, 0:width]) * (SCALE2 * 64 ** (-0.5))
        for p in range(pairs):
            qt_ref[p] = block[:, p * LANES : (p + 1) * LANES].astype(jnp.bfloat16).T

            @pl.when(helped)
            def _():
                query_back(p).start()

    def keys():
        block = f32dot(h_s[...], w2_ref[:, width : 2 * width]).astype(jnp.bfloat16)
        for p in range(pairs):
            k_ref[0, p] = block[:, p * LANES : (p + 1) * LANES]

    def values():
        block = f32dot(h_s[...], w2_ref[:, 2 * width : 3 * width])
        for p in range(pairs):
            v_ref[0, p] = block[:, p * LANES : (p + 1) * LANES].astype(jnp.bfloat16).T

    @pl.when(jnp.logical_not(hands_on))
    def _():
        queries()
        keys()
        sib[0].start()
        values()
        sib[1].start()

    @pl.when(hands_on)
    def _():
        keys()
        keys_on().start()
        sib[0].start()
        values()
        for p in range(pairs):
            values_on(p).start()

        sib[1].start()
        queries()

    half_rows = LANES // 2
    blank = jnp.zeros((half_rows, rows), jnp.bfloat16)

    def pair_attend(p, query, slots, biases, put):
        def score(side):
            own = query[side * half_rows : (side + 1) * half_rows, :]
            mine = jnp.concatenate([own, blank] if side == 0 else [blank, own], axis=0)
            tops = []
            for j, slot in enumerate(slots):
                s = f32dot(k_ref[slot, p], mine)
                s_s[side * 3 + j] = s
                tops.append(jnp.max(s, axis=0, keepdims=True))
            best = functools.reduce(
                jnp.maximum, [top + bias for top, bias in zip(tops, biases)]
            )
            return best, [jnp.maximum(best - bias, top) for top, bias in zip(tops, biases)]

        def soft(side, best, refs):
            total, acc = None, None
            for j, slot in enumerate(slots):
                w = jnp.exp2(s_s[side * 3 + j] - refs[j])
                add = jnp.sum(w, axis=0, keepdims=True)
                part = f32dot(
                    v_ref[slot, p, side * half_rows : (side + 1) * half_rows, :],
                    w.astype(jnp.bfloat16),
                )
                total = add if total is None else total + add
                acc = part if acc is None else acc + part
            put(p, side, best, total, acc)

        first = score(0)
        second = score(1)
        soft(0, *first)
        soft(1, *second)

    def put_merged(p, side, best, total, acc):
        arow = slice(side * half_rows, (side + 1) * half_rows)
        m_old = m_s[p, side]
        m_new = jnp.maximum(m_old, best)
        alpha, beta = jnp.exp2(m_old - m_new), jnp.exp2(best - m_new)
        m_s[p, side] = m_new
        l_s[p, side] = l_s[p, side] * alpha + total * beta
        acc_s[p, arow, :] = acc_s[p, arow, :] * alpha + acc * beta

    def put_far(p, side, best, total, acc):
        some = total > 0.0
        inv = jnp.where(some, 1.0 / total, 0.0)
        st_send[p, side : side + 1, :] = jnp.where(some, best + jnp.log2(total), FAR)
        o_send[p, side * half_rows : (side + 1) * half_rows, :] = (acc * inv).astype(jnp.bfloat16)

    def loop_pairs(body):
        def step(p, carry):
            body(p)
            return carry

        lax.fori_loop(0, pairs, step, 0)

    own_mask = lax.broadcasted_iota(jnp.int32, (half, half), 0) <= (
        lax.broadcasted_iota(jnp.int32, (half, half), 1)
    )

    def own_attend(p):
        query = qt_ref[p]

        def score(side):
            own = query[side * half_rows : (side + 1) * half_rows, :]
            mine = jnp.concatenate([own, blank] if side == 0 else [blank, own], axis=0)
            s = f32dot(k_ref[0, p, 0:half, :], mine)
            left, right = jnp.where(own_mask, s[:, 0:half], FAR), s[:, half:rows]
            low_right = f32dot(k_ref[0, p, half:rows, :], mine[:, half:rows])
            low_right = jnp.where(own_mask, low_right, FAR)
            s_s[side, 0:half, 0:half] = left
            s_s[side, 0:half, half:rows] = right
            s_s[side, half:rows, half:rows] = low_right
            top = jnp.maximum(
                jnp.max(right, axis=0, keepdims=True), jnp.max(low_right, axis=0, keepdims=True)
            )
            return jnp.concatenate([jnp.max(left, axis=0, keepdims=True), top], axis=1)

        def soft(side, best):
            arow = slice(side * half_rows, (side + 1) * half_rows)
            w = jnp.exp2(s_s[side, 0:half, :] - best)
            late = jnp.exp2(s_s[side, half:rows, half:rows] - best[:, half:rows])
            total = jnp.sum(w, axis=0, keepdims=True)
            part = f32dot(v_ref[0, p, arow, 0:half], w.astype(jnp.bfloat16))
            more = f32dot(v_ref[0, p, arow, half:rows], late.astype(jnp.bfloat16))
            m_s[p, side] = best
            l_s[p, side, :, 0:half] = total[:, 0:half]
            l_s[p, side, :, half:rows] = total[:, half:rows] + jnp.sum(late, axis=0, keepdims=True)
            acc_s[p, arow, 0:half] = part[:, 0:half]
            acc_s[p, arow, half:rows] = part[:, half:rows] + more

        tops = [score(side) for side in range(2)]
        for side in range(2):
            soft(side, tops[side])

    loop_pairs(own_attend)
    for copy in sib:
        copy.wait_recv()

    def help_bias(j):
        return bias_recv[j : j + 1, 0:1]

    def give(p):
        for copy in partial_on(p):
            copy.start()

    def near_part(p, put):
        query_back(p).wait_recv()
        pair_attend(p, q_far[p], [0, 1], [help_bias(0), help_bias(1)], put)

    @pl.when(helps)
    def _():
        bias_back().wait_recv()

    @pl.when(gets_prev)
    def _():
        keys_on().wait_recv()
        biases = [help_bias(j) for j in range(3)]

        def body(p):
            query_back(p).wait_recv()
            values_on(p).wait_recv()
            pair_attend(p, q_far[p], [0, 1, 2], biases, put_far)
            give(p)

        loop_pairs(body)

    @pl.when(jnp.logical_and(even, jnp.logical_and(helps, jnp.logical_not(gets_prev))))
    def _():
        def body(p):
            near_part(p, put_far)
            give(p)

        loop_pairs(body)

    @pl.when(odd)
    def _():
        bias = listing(1)

        @pl.when(helps)
        def _():
            def body(p):
                near_part(p, put_far)
                give(p)

            loop_pairs(body)

        loop_pairs(lambda p: pair_attend(p, qt_ref[p], [1], [bias], put_merged))

    def most_of_output(j, carry):
        cols = tile_at(j, WIDE)
        most = (pairs - 1) * LANES
        sum_ref[:, cols] = hid_ref[:, cols].astype(jnp.float32) + f32dot(
            y_s[:, 0:most], wp_ref[0:most, cols]
        )
        return carry

    for p in range(pairs):
        @pl.when(helped)
        def _():
            for copy in partial_on(p):
                copy.wait_recv()
            for half in range(2):
                far = o_recv[p, half * half_rows : (half + 1) * half_rows, :]
                put_merged(
                    p, half, st_recv[p, half : half + 1, :], 1.0, far.astype(jnp.float32),
                )

        whole = jnp.concatenate(
            [
                acc_s[p, 0:half_rows, :] * (1.0 / l_s[p, 0]),
                acc_s[p, half_rows:LANES, :] * (1.0 / l_s[p, 1]),
            ],
            axis=0,
        )
        if p < pairs - 1:
            y_s[:, p * LANES : (p + 1) * LANES] = whole.T.astype(jnp.bfloat16)
        else:
            y_last[...] = whole.T.astype(jnp.bfloat16)
        if p == pairs - 2:
            loads[5].wait()
            lax.fori_loop(0, hid_ref.shape[1] // WIDE, most_of_output, 0)

    def drain(copies):
        for copy in copies:
            copy.wait_send()

    for r, dist in enumerate(dists):
        @pl.when(me + dist < n)
        def _():
            for copy in copy_of(r, dist):
                copy.wait_send()

    drain(sib)

    @pl.when(hands_on)
    def _():
        drain([keys_on()] + [values_on(p) for p in range(pairs)])

    @pl.when(helped)
    def _():
        drain([bias_back()])

    for p in range(pairs):
        @pl.when(helped)
        def _():
            drain([query_back(p)])

        @pl.when(helps)
        def _():
            drain(partial_on(p))


def close_layer(y_ref, sum_ref, wp_ref, out_hbm, out_ref, sems):
    copies = []
    for i in range(out_ref.shape[0] // LANES):
        rows = slice(i * LANES, (i + 1) * LANES)
        branch = f32dot(y_ref[rows, :], wp_ref[wp_ref.shape[0] - LANES :, :])
        out_ref[rows, :] = (sum_ref[rows, :] + branch).astype(jnp.bfloat16)
        copies.append(pltpu.make_async_copy(out_ref.at[rows], out_hbm.at[rows], sems.at[i]))
        copies[-1].start()
    for copy in copies:
        copy.wait()


def in_vmem(array):
    return pltpu.with_memory_space_constraint(array, pltpu.VMEM)


def local(
    frames, norm_gain1, w_qkv1, log_decay, head_gain, w_out1, norm_gain2, w_qkv2, window_ids, w_out2
):
    n = lax.axis_size("tm")
    rows, model = frames.shape
    width = w_out1.shape[0]
    heads = log_decay.shape[0]
    rounds = max(2, (n - 1).bit_length())
    pairs = width // LANES
    vmem = pl.BlockSpec(memory_space=pltpu.VMEM)
    hbm = pl.BlockSpec(memory_space=pltpu.HBM)
    bf, f32 = jnp.bfloat16, jnp.float32
    last, most = pl.pallas_call(
        functools.partial(both_layers, n),
        out_shape=[
            pltpu.VMEM((rows, LANES), bf),
            pltpu.VMEM((rows, model), f32),
        ],
        in_specs=[hbm] * 10,
        out_specs=[vmem, vmem],
        scratch_shapes=[
            pltpu.VMEM((1, model), f32),
            pltpu.VMEM((heads, rows), f32),
            pltpu.VMEM((1, width), f32),
            pltpu.VMEM((1, model), f32),
            pltpu.SMEM(window_ids.shape, jnp.int32),
            pltpu.SemaphoreType.DMA((5,)),
            pltpu.VMEM((width, model), bf),
            pltpu.VMEM((rows, model), bf),
            pltpu.VMEM((rows, model), bf),
            pltpu.VMEM((model, 3 * width), bf),
            pltpu.VMEM((width, model), bf),
            pltpu.VMEM((model, 3 * width), bf),
            pltpu.VMEM((pairs, LANES, rows), bf),
            pltpu.VMEM((pairs, LANES, rows), bf),
            pltpu.VMEM((3, pairs, rows, LANES), bf),
            pltpu.VMEM((3, pairs, LANES, rows), bf),
            pltpu.VMEM((pairs, 2, 1, rows), f32),
            pltpu.VMEM((pairs, 2, 1, rows), f32),
            pltpu.VMEM((pairs, LANES, rows), f32),
            pltpu.VMEM((6, rows, rows), f32),
            pltpu.VMEM((pairs, LANES, rows), bf),
            pltpu.VMEM((pairs, LANES, rows), bf),
            pltpu.VMEM((pairs, 2, rows), f32),
            pltpu.VMEM((pairs, 2, rows), f32),
            pltpu.VMEM((8, LANES), f32),
            pltpu.VMEM((8, LANES), f32),
            pltpu.SemaphoreType.DMA((6,)),
            pltpu.SemaphoreType.DMA((2,)),
            pltpu.SemaphoreType.DMA((2,)),
            pltpu.SemaphoreType.DMA((pairs + 1,)),
            pltpu.SemaphoreType.DMA((pairs + 1,)),
            pltpu.SemaphoreType.DMA((pairs, 3)),
            pltpu.SemaphoreType.DMA((pairs, 3)),
            pltpu.SemaphoreType.DMA((2,)),
            pltpu.VMEM((rows, model), bf),
            pltpu.VMEM((rows, 3 * width), bf),
            pltpu.VMEM((rows, width), bf),
            pltpu.VMEM((heads, rows), f32),
            pltpu.VMEM((rows, heads), f32),
            pltpu.VMEM((rows, width), f32),
            pltpu.VMEM((64, width), f32),
            pltpu.VMEM((heads, LANES), f32),
            pltpu.VMEM((64, width), f32),
            pltpu.VMEM((64, width), f32),
            pltpu.VMEM((heads, LANES), f32),
            pltpu.VMEM((rounds, 64, width), bf),
            pltpu.VMEM((rounds, 64, width), bf),
            pltpu.VMEM((rounds, heads, LANES), f32),
            pltpu.VMEM((rounds, heads, LANES), f32),
            pltpu.SemaphoreType.DMA((rounds, 2)),
            pltpu.SemaphoreType.DMA((rounds, 2)),
        ],
        compiler_params=pltpu.CompilerParams(
            collective_id=0, has_side_effects=True, vmem_limit_bytes=60 * 2**20
        ),
    )(
        frames, norm_gain1.reshape(1, model), w_qkv1, log_decay, head_gain.reshape(1, width),
        w_out1, norm_gain2.reshape(1, model), w_qkv2, window_ids, w_out2,
    )
    parts = rows // LANES
    return pl.pallas_call(
        close_layer,
        out_shape=jax.ShapeDtypeStruct((rows, model), bf),
        in_specs=[vmem, vmem, vmem],
        out_specs=hbm,
        scratch_shapes=[
            pltpu.VMEM((rows, model), bf),
            pltpu.SemaphoreType.DMA((parts,)),
        ],
        compiler_params=pltpu.CompilerParams(vmem_limit_bytes=8 * 2**20),
    )(in_vmem(last), in_vmem(most), in_vmem(w_out2))


def solution(mesh):
    placed = (
        P(("dp", "tm"), None),
        P(),
        P(),
        P(None, ("dp", "tm")),
        P(),
        P(),
        P(),
        P(),
        P(("dp", "tm"), None),
        P(),
    )
    return jax.shard_map(
        local, mesh=mesh, in_specs=placed, out_specs=P(("dp", "tm"), None), check_vma=False
    )
```

```python
import functools

import jax
import jax.numpy as jnp
from jax import lax
from jax.experimental import pallas as pl
from jax.experimental.pallas import tpu as pltpu
from jax.sharding import PartitionSpec as P

MESH = pl.DeviceIdType.MESH
TILE = 256
WIDE = 512
FAR = -1e30
LANES = 128
SCALE2 = 1.4426950408889634


def f32dot(a, b, dims=(((1,), (0,)), ((), ()))):
    return lax.dot_general(a, b, dims, preferred_element_type=jnp.float32)


def tile_at(index, size):
    return pl.ds(pl.multiple_of(index * size, size), size)


def norm_rows(src_ref, gain_ref, dst_ref):
    step = 256

    def body(i, carry):
        rows = tile_at(i, step)
        wide = src_ref[rows, :].astype(jnp.float32)
        scale = lax.rsqrt(jnp.mean(wide * wide, axis=-1, keepdims=True) + 1e-05)
        dst_ref[rows, :] = (wide * scale * gain_ref[...]).astype(jnp.bfloat16)
        return carry

    lax.fori_loop(0, src_ref.shape[0] // step, body, 0)


def both_layers(
    n,
    x_hbm, g1_hbm, w1_hbm, ld_hbm, hg_hbm, wo_hbm, g2_hbm, w2_hbm, ids_hbm, wp_hbm,
    y_last, sum_ref,
    g1_ref, ld_ref, hg_ref, g2_ref, ids_ref, small_sem,
    wp_ref, hid_ref,
    x_ref, w1_ref, wo_ref, w2_ref, qt_ref, q_far, k_ref, v_ref,
    m_s, l_s, acc_s, s_s, o_send, o_recv, st_send, st_recv, bias_send, bias_recv,
    load_sem, kv_send, kv_recv, on_send, on_recv, far_send, far_recv, bias_sems,
    h_s, qkv_s, y_s, run_s, runt_s, lin_s, x_s, ax_s, e_s, em_s, a_s, send_b, recv_b, send_a, recv_a, send_sem, recv_sem,
):
    me = lax.axis_index("tm")
    small = [
        pltpu.make_async_copy(src, dst, small_sem.at[i])
        for i, (src, dst) in enumerate(
            [(ld_hbm, ld_ref), (g1_hbm, g1_ref), (hg_hbm, hg_ref), (g2_hbm, g2_ref), (ids_hbm, ids_ref)]
        )
    ]
    x_load = pltpu.make_async_copy(x_hbm, x_ref, load_sem.at[0])
    x_load.start()
    for load in small:
        load.start()
    rows = x_ref.shape[0]
    width = wo_ref.shape[0]
    heads = ld_ref.shape[0]
    pairs = width // LANES
    rounds = max(2, (n - 1).bit_length())
    dists = [1 << r for r in range(rounds)]

    barrier = pltpu.get_barrier_semaphore()
    for dist in dists:
        @pl.when(me + dist < n)
        def _():
            pl.semaphore_signal(barrier, inc=1, device_id={"tm": me + dist}, device_id_type=MESH)

        @pl.when(me >= dist)
        def _():
            pl.semaphore_signal(barrier, inc=1, device_id={"tm": me - dist}, device_id_type=MESH)

    loads = [
        pltpu.make_async_copy(src, dst, load_sem.at[i])
        for i, (src, dst) in enumerate(
            [
                (x_hbm, x_ref),
                (w1_hbm.at[:, width:], w1_ref.at[:, width:]),
                (w1_hbm.at[:, :width], w1_ref.at[:, :width]),
                (wo_hbm, wo_ref),
                (w2_hbm, w2_ref),
                (wp_hbm, wp_ref),
            ]
        )
    ]
    for load in loads[1:]:
        load.start()
    for load in small:
        load.wait()
    upper = (
        lax.broadcasted_iota(jnp.int32, (rows, rows), 0)
        <= lax.broadcasted_iota(jnp.int32, (rows, rows), 1)
    ).astype(jnp.float32)
    run = lax.dot_general(
        ld_ref[...], upper, (((1,), (0,)), ((), ())),
        precision=lax.Precision.HIGHEST, preferred_element_type=jnp.float32,
    )
    run_s[...] = run
    runt_s[...] = run.T
    last = run[:, rows - 1 : rows]
    headsel = lax.broadcasted_iota(jnp.int32, (heads, width), 1) // (
        width // heads
    ) == lax.broadcasted_iota(jnp.int32, (heads, width), 0)
    def by_lane(per_head):
        return jnp.sum(jnp.where(headsel, per_head[:, 0:1], 0.0), axis=0, keepdims=True)

    a_s[...] = jnp.broadcast_to(jnp.exp(last), a_s.shape)
    low = lax.broadcasted_iota(jnp.int32, (1, LANES), 1) < LANES // 2
    keeps = [jnp.where(low, 1.0 - side, float(side)).astype(jnp.bfloat16) for side in range(2)]
    half = rows // 2
    mid = run[:, half - 1 : half]
    early = lax.broadcasted_iota(jnp.int32, (heads, rows), 1) < half
    left_t = jnp.exp(jnp.where(early, mid, last) - run).T
    runt_s[half:rows, :] = runt_s[half:rows, :] - runt_s[half - 1 : half, :]
    run_s[...] = jnp.where(early, run, run - mid)
    mid_row, rest_row = by_lane(jnp.exp(mid)), by_lane(jnp.exp(last - mid))

    loads[0].wait()
    norm_rows(x_ref, g1_ref, h_s)
    loads[1].wait()

    def project(j, carry):
        cols = tile_at(j, WIDE)
        qkv_s[:, cols] = f32dot(h_s[...], w1_ref[:, cols]).astype(jnp.bfloat16)
        return carry

    for j in range(2):
        cols = slice(width * (j + 1), width * (j + 2))
        qkv_s[:, cols] = f32dot(h_s[...], w1_ref[:, cols]).astype(jnp.bfloat16)

    for p in range(pairs):
        cols = slice(p * LANES, (p + 1) * LANES)
        kcols = slice(width + p * LANES, width + (p + 1) * LANES)
        vcols = slice(2 * width + p * LANES, 2 * width + (p + 1) * LANES)
        decay = jnp.where(low, left_t[:, 2 * p : 2 * p + 1], left_t[:, 2 * p + 1 : 2 * p + 2])
        keyed = (qkv_s[:, kcols].astype(jnp.float32) * decay).astype(jnp.bfloat16).T
        ends = []
        for first in (0, half):
            full = f32dot(keyed[:, first : first + half], qkv_s[first : first + half, vcols])
            ends.append(jnp.where(low, full[: LANES // 2], full[LANES // 2 :]))
        em_s[:, cols] = ends[0]
        e_s[:, cols] = ends[0] * rest_row[:, cols] + ends[1]
    x_s[...] = jnp.zeros_like(x_s)
    ax_s[...] = jnp.ones_like(ax_s)

    def send(r, dist):
        @pl.when(me + dist < n)
        def _():
            send_b[r] = (e_s[...] + by_lane(a_s[...]) * x_s[...]).astype(jnp.bfloat16)
            send_a[r] = a_s[...] * ax_s[...]
            for copy in copy_of(r, dist):
                copy.start()

    def copy_of(r, dist):
        return [
            pltpu.make_async_remote_copy(
                src_ref=src.at[r], dst_ref=dst.at[r],
                send_sem=send_sem.at[r, i], recv_sem=recv_sem.at[r, i],
                device_id={"tm": me + dist}, device_id_type=MESH,
            )
            for i, (src, dst) in enumerate([(send_b, recv_b), (send_a, recv_a)])
        ]

    def receive(r, dist):
        @pl.when(me >= dist)
        def _():
            for copy in copy_of(r, dist):
                copy.wait_recv()
            x_s[...] = x_s[...] + by_lane(ax_s[...]) * recv_b[r].astype(jnp.float32)
            ax_s[...] = ax_s[...] * recv_a[r]

    peers = [me + dist < n for dist in dists] + [me >= dist for dist in dists]
    pl.semaphore_wait(barrier, sum(peer.astype(jnp.int32) for peer in peers))

    core = lax.rem(me, 2)
    even = core == 0
    odd = jnp.logical_not(even)
    helps = me + 2 < n
    helped = me >= 2
    hands_on = jnp.logical_and(odd, me + 3 < n)
    gets_prev = jnp.logical_and(even, jnp.logical_and(me >= 2, helps))

    def listing(back):
        listed = ids_ref[0, 0] == me - back
        for j in range(1, ids_ref.shape[1]):
            listed = jnp.logical_or(listed, ids_ref[0, j] == me - back)
        return jnp.where(listed, jnp.float32(0.0), jnp.float32(FAR))

    def bias_back():
        return pltpu.make_async_remote_copy(
            src_ref=bias_send, dst_ref=bias_recv,
            send_sem=bias_sems.at[0], recv_sem=bias_sems.at[1],
            device_id={"tm": me - 2}, device_id_type=MESH,
        )

    near = jnp.where(even, listing(1), listing(3))
    brow = lax.broadcasted_iota(jnp.int32, bias_send.shape, 0)
    bias_send[...] = jnp.where(brow == 0, listing(2), jnp.where(brow == 1, near, listing(3)))

    @pl.when(helped)
    def _():
        bias_back().start()

    def work_query():
        loads[2].wait()
        lax.fori_loop(0, width // WIDE, project, 0)

    def work_pair(p):
        cols = slice(p * LANES, (p + 1) * LANES)
        kcols = slice(width + p * LANES, width + (p + 1) * LANES)
        vcols = slice(2 * width + p * LANES, 2 * width + (p + 1) * LANES)
        causal = lax.broadcasted_iota(jnp.int32, (half, half), 0) >= (
            lax.broadcasted_iota(jnp.int32, (half, half), 1)
        )
        blocks = [(first, side) for first in range(0, rows, half) for side in range(2)]
        scores = []
        for first, side in blocks:
            scores.append(
                f32dot(
                    qkv_s[first : first + half, cols] * keeps[side],
                    qkv_s[first : first + half, kcols], (((1,), (1,)), ((), ())),
                )
            )
        parts = []
        for (first, side), score in zip(blocks, scores):
            h = 2 * p + side
            diff = runt_s[first : first + half, h : h + 1] - run_s[h : h + 1, first : first + half]
            weight = jnp.exp(jnp.where(causal, jnp.minimum(diff, 0.0), FAR))
            parts.append(
                f32dot((score * weight).astype(jnp.bfloat16), qkv_s[first : first + half, vcols])
            )
        for i, first in enumerate(range(0, rows, half)):
            lin_s[first : first + half, cols] = jnp.where(low, parts[2 * i], parts[2 * i + 1])

    work = [work_query] + [functools.partial(work_pair, p) for p in range(pairs)]
    def send_after(r):
        if r < rounds:
            @pl.when(me >= (dists[r - 1] if r else 0))
            def _():
                send(r, dists[r])

        if r + 1 < rounds:
            @pl.when(jnp.logical_and(me >= (dists[r - 1] if r else 0), me < dists[r]))
            def _():
                for later in range(r + 1, rounds):
                    send(later, dists[later])

    send_after(0)
    for r, dist in enumerate(dists):
        take = 1 if r == 0 else len(work)
        for item in work[:take]:
            item()
        work = work[take:]
        receive(r, dist)
        send_after(r + 1)
    for item in work:
        item()

    side_of = [lax.broadcasted_iota(jnp.int32, (LANES, LANES), d) // 64 for d in (0, 1)]
    same_head = (side_of[0] == side_of[1]).astype(jnp.float32).astype(jnp.bfloat16)
    for p in range(pairs):
        cols = slice(p * LANES, (p + 1) * LANES)
        grow = jnp.exp(
            jnp.where(low, runt_s[:, 2 * p : 2 * p + 1], runt_s[:, 2 * p + 1 : 2 * p + 2])
        )
        scaled = (qkv_s[:, cols].astype(jnp.float32) * grow).astype(jnp.bfloat16)
        before = x_s[:, cols]
        inter = []
        for first, packed in ((0, before), (half, before * mid_row[:, cols] + em_s[:, cols])):
            state = jnp.concatenate(
                [jnp.where(low, packed, 0.0), jnp.where(low, 0.0, packed)], axis=0
            ).astype(jnp.bfloat16)
            inter.append(f32dot(scaled[first : first + half], state))
        lin = lin_s[:, cols] + jnp.concatenate(inter, axis=0)
        square = lin * lin
        high = square.astype(jnp.bfloat16)
        rest = (square - high.astype(jnp.float32)).astype(jnp.bfloat16)
        mean = (f32dot(high, same_head) + f32dot(rest, same_head)) * (1.0 / 64)
        y_s[:, cols] = (lin * lax.rsqrt(mean + 1e-06) * hg_ref[:, cols]).astype(jnp.bfloat16)

    loads[3].wait()
    for j in range(x_ref.shape[1] // WIDE):
        cols = slice(j * WIDE, (j + 1) * WIDE)
        branch = f32dot(y_s[...], wo_ref[:, cols])
        hid_ref[:, cols] = (x_ref[:, cols].astype(jnp.float32) + branch).astype(jnp.bfloat16)
    loads[4].wait()
    norm_rows(hid_ref, g2_ref, h_s)

    def query_back(p):
        return pltpu.make_async_remote_copy(
            src_ref=qt_ref.at[p], dst_ref=q_far.at[p],
            send_sem=far_send.at[p, 0], recv_sem=far_recv.at[p, 0],
            device_id={"tm": me - 2}, device_id_type=MESH,
        )

    def partial_on(p):
        return [
            pltpu.make_async_remote_copy(
                src_ref=src.at[p], dst_ref=dst.at[p],
                send_sem=far_send.at[p, i], recv_sem=far_recv.at[p, i],
                device_id={"tm": me + 2}, device_id_type=MESH,
            )
            for i, (src, dst) in [(1, (o_send, o_recv)), (2, (st_send, st_recv))]
        ]

    sib = [
        pltpu.make_async_remote_copy(
            src_ref=ref.at[0], dst_ref=ref.at[1],
            send_sem=kv_send.at[i], recv_sem=kv_recv.at[i],
            device_id={"tm": me + 1 - 2 * core}, device_id_type=MESH,
        )
        for i, ref in enumerate([k_ref, v_ref])
    ]

    def keys_on():
        return pltpu.make_async_remote_copy(
            src_ref=k_ref.at[0], dst_ref=k_ref.at[2],
            send_sem=on_send.at[pairs], recv_sem=on_recv.at[pairs],
            device_id={"tm": me + 1}, device_id_type=MESH,
        )

    def values_on(p):
        return pltpu.make_async_remote_copy(
            src_ref=v_ref.at[0, p], dst_ref=v_ref.at[2, p],
            send_sem=on_send.at[p], recv_sem=on_recv.at[p],
            device_id={"tm": me + 1}, device_id_type=MESH,
        )

    def queries():
        block = f32dot(h_s[...], w2_ref[:, 0:width]) * (SCALE2 * 64 ** (-0.5))
        for p in range(pairs):
            qt_ref[p] = block[:, p * LANES : (p + 1) * LANES].astype(jnp.bfloat16).T

            @pl.when(helped)
            def _():
                query_back(p).start()

    def keys():
        block = f32dot(h_s[...], w2_ref[:, width : 2 * width]).astype(jnp.bfloat16)
        for p in range(pairs):
            k_ref[0, p] = block[:, p * LANES : (p + 1) * LANES]

    def values():
        block = f32dot(h_s[...], w2_ref[:, 2 * width : 3 * width])
        for p in range(pairs):
            v_ref[0, p] = block[:, p * LANES : (p + 1) * LANES].astype(jnp.bfloat16).T

    @pl.when(jnp.logical_not(hands_on))
    def _():
        queries()
        keys()
        sib[0].start()
        values()
        sib[1].start()

    @pl.when(hands_on)
    def _():
        keys()
        keys_on().start()
        sib[0].start()
        values()
        for p in range(pairs):
            values_on(p).start()

        sib[1].start()
        queries()

    half_rows = LANES // 2
    blank = jnp.zeros((half_rows, rows), jnp.bfloat16)

    def pair_attend(p, query, slots, biases, put):
        def score(side):
            own = query[side * half_rows : (side + 1) * half_rows, :]
            mine = jnp.concatenate([own, blank] if side == 0 else [blank, own], axis=0)
            tops = []
            for j, slot in enumerate(slots):
                s = f32dot(k_ref[slot, p], mine)
                s_s[side * 3 + j] = s
                tops.append(jnp.max(s, axis=0, keepdims=True))
            best = functools.reduce(
                jnp.maximum, [top + bias for top, bias in zip(tops, biases)]
            )
            return best, [jnp.maximum(best - bias, top) for top, bias in zip(tops, biases)]

        def soft(side, best, refs):
            total, acc = None, None
            for j, slot in enumerate(slots):
                w = jnp.exp2(s_s[side * 3 + j] - refs[j])
                add = jnp.sum(w, axis=0, keepdims=True)
                part = f32dot(
                    v_ref[slot, p, side * half_rows : (side + 1) * half_rows, :],
                    w.astype(jnp.bfloat16),
                )
                total = add if total is None else total + add
                acc = part if acc is None else acc + part
            put(p, side, best, total, acc)

        first = score(0)
        second = score(1)
        soft(0, *first)
        soft(1, *second)

    def put_merged(p, side, best, total, acc):
        arow = slice(side * half_rows, (side + 1) * half_rows)
        m_old = m_s[p, side]
        m_new = jnp.maximum(m_old, best)
        alpha, beta = jnp.exp2(m_old - m_new), jnp.exp2(best - m_new)
        m_s[p, side] = m_new
        l_s[p, side] = l_s[p, side] * alpha + total * beta
        acc_s[p, arow, :] = acc_s[p, arow, :] * alpha + acc * beta

    def put_far(p, side, best, total, acc):
        some = total > 0.0
        inv = jnp.where(some, 1.0 / total, 0.0)
        st_send[p, side : side + 1, :] = jnp.where(some, best + jnp.log2(total), FAR)
        o_send[p, side * half_rows : (side + 1) * half_rows, :] = (acc * inv).astype(jnp.bfloat16)

    def loop_pairs(body):
        def step(p, carry):
            body(p)
            return carry

        lax.fori_loop(0, pairs, step, 0)

    own_mask = lax.broadcasted_iota(jnp.int32, (half, half), 0) <= (
        lax.broadcasted_iota(jnp.int32, (half, half), 1)
    )

    def own_attend(p):
        query = qt_ref[p]

        def score(side):
            own = query[side * half_rows : (side + 1) * half_rows, :]
            mine = jnp.concatenate([own, blank] if side == 0 else [blank, own], axis=0)
            s = f32dot(k_ref[0, p, 0:half, :], mine)
            left, right = jnp.where(own_mask, s[:, 0:half], FAR), s[:, half:rows]
            low_right = f32dot(k_ref[0, p, half:rows, :], mine[:, half:rows])
            low_right = jnp.where(own_mask, low_right, FAR)
            s_s[side, 0:half, 0:half] = left
            s_s[side, 0:half, half:rows] = right
            s_s[side, half:rows, half:rows] = low_right
            top = jnp.maximum(
                jnp.max(right, axis=0, keepdims=True), jnp.max(low_right, axis=0, keepdims=True)
            )
            return jnp.concatenate([jnp.max(left, axis=0, keepdims=True), top], axis=1)

        def soft(side, best):
            arow = slice(side * half_rows, (side + 1) * half_rows)
            w = jnp.exp2(s_s[side, 0:half, :] - best)
            late = jnp.exp2(s_s[side, half:rows, half:rows] - best[:, half:rows])
            total = jnp.sum(w, axis=0, keepdims=True)
            part = f32dot(v_ref[0, p, arow, 0:half], w.astype(jnp.bfloat16))
            more = f32dot(v_ref[0, p, arow, half:rows], late.astype(jnp.bfloat16))
            m_s[p, side] = best
            l_s[p, side, :, 0:half] = total[:, 0:half]
            l_s[p, side, :, half:rows] = total[:, half:rows] + jnp.sum(late, axis=0, keepdims=True)
            acc_s[p, arow, 0:half] = part[:, 0:half]
            acc_s[p, arow, half:rows] = part[:, half:rows] + more

        tops = [score(side) for side in range(2)]
        for side in range(2):
            soft(side, tops[side])

    loop_pairs(own_attend)
    for copy in sib:
        copy.wait_recv()

    def help_bias(j):
        return bias_recv[j : j + 1, 0:1]

    def give(p):
        for copy in partial_on(p):
            copy.start()

    def near_part(p, put):
        query_back(p).wait_recv()
        pair_attend(p, q_far[p], [0, 1], [help_bias(0), help_bias(1)], put)

    @pl.when(helps)
    def _():
        bias_back().wait_recv()

    @pl.when(gets_prev)
    def _():
        keys_on().wait_recv()
        biases = [help_bias(j) for j in range(3)]

        def body(p):
            query_back(p).wait_recv()
            values_on(p).wait_recv()
            pair_attend(p, q_far[p], [0, 1, 2], biases, put_far)
            give(p)

        loop_pairs(body)

    @pl.when(jnp.logical_and(even, jnp.logical_and(helps, jnp.logical_not(gets_prev))))
    def _():
        def body(p):
            near_part(p, put_far)
            give(p)

        loop_pairs(body)

    @pl.when(odd)
    def _():
        bias = listing(1)

        @pl.when(helps)
        def _():
            def body(p):
                near_part(p, put_far)
                give(p)

            loop_pairs(body)

        loop_pairs(lambda p: pair_attend(p, qt_ref[p], [1], [bias], put_merged))

    def most_of_output(j, carry):
        cols = tile_at(j, WIDE)
        most = (pairs - 1) * LANES
        sum_ref[:, cols] = hid_ref[:, cols].astype(jnp.float32) + f32dot(
            y_s[:, 0:most], wp_ref[0:most, cols]
        )
        return carry

    for p in range(pairs):
        @pl.when(helped)
        def _():
            for copy in partial_on(p):
                copy.wait_recv()
            for half in range(2):
                far = o_recv[p, half * half_rows : (half + 1) * half_rows, :]
                put_merged(
                    p, half, st_recv[p, half : half + 1, :], 1.0, far.astype(jnp.float32),
                )

        whole = jnp.concatenate(
            [
                acc_s[p, 0:half_rows, :] * (1.0 / l_s[p, 0]),
                acc_s[p, half_rows:LANES, :] * (1.0 / l_s[p, 1]),
            ],
            axis=0,
        )
        if p < pairs - 1:
            y_s[:, p * LANES : (p + 1) * LANES] = whole.T.astype(jnp.bfloat16)
        else:
            y_last[...] = whole.T.astype(jnp.bfloat16)
        if p == pairs - 2:
            loads[5].wait()
            lax.fori_loop(0, hid_ref.shape[1] // WIDE, most_of_output, 0)

    def drain(copies):
        for copy in copies:
            copy.wait_send()

    for r, dist in enumerate(dists):
        @pl.when(me + dist < n)
        def _():
            for copy in copy_of(r, dist):
                copy.wait_send()

    drain(sib)

    @pl.when(hands_on)
    def _():
        drain([keys_on()] + [values_on(p) for p in range(pairs)])

    @pl.when(helped)
    def _():
        drain([bias_back()])

    for p in range(pairs):
        @pl.when(helped)
        def _():
            drain([query_back(p)])

        @pl.when(helps)
        def _():
            drain(partial_on(p))


def close_layer(y_ref, sum_ref, wp_ref, out_hbm, out_ref, sems):
    copies = []
    for i in range(out_ref.shape[0] // LANES):
        rows = slice(i * LANES, (i + 1) * LANES)
        branch = f32dot(y_ref[rows, :], wp_ref[wp_ref.shape[0] - LANES :, :])
        out_ref[rows, :] = (sum_ref[rows, :] + branch).astype(jnp.bfloat16)
        copies.append(pltpu.make_async_copy(out_ref.at[rows], out_hbm.at[rows], sems.at[i]))
        copies[-1].start()
    for copy in copies:
        copy.wait()


def in_vmem(array):
    return pltpu.with_memory_space_constraint(array, pltpu.VMEM)


def local(
    frames, norm_gain1, w_qkv1, log_decay, head_gain, w_out1, norm_gain2, w_qkv2, window_ids, w_out2
):
    n = lax.axis_size("tm")
    rows, model = frames.shape
    width = w_out1.shape[0]
    heads = log_decay.shape[0]
    rounds = max(2, (n - 1).bit_length())
    pairs = width // LANES
    vmem = pl.BlockSpec(memory_space=pltpu.VMEM)
    hbm = pl.BlockSpec(memory_space=pltpu.HBM)
    bf, f32 = jnp.bfloat16, jnp.float32
    last, most = pl.pallas_call(
        functools.partial(both_layers, n),
        out_shape=[
            pltpu.VMEM((rows, LANES), bf),
            pltpu.VMEM((rows, model), f32),
        ],
        in_specs=[hbm] * 10,
        out_specs=[vmem, vmem],
        scratch_shapes=[
            pltpu.VMEM((1, model), f32),
            pltpu.VMEM((heads, rows), f32),
            pltpu.VMEM((1, width), f32),
            pltpu.VMEM((1, model), f32),
            pltpu.SMEM(window_ids.shape, jnp.int32),
            pltpu.SemaphoreType.DMA((5,)),
            pltpu.VMEM((width, model), bf),
            pltpu.VMEM((rows, model), bf),
            pltpu.VMEM((rows, model), bf),
            pltpu.VMEM((model, 3 * width), bf),
            pltpu.VMEM((width, model), bf),
            pltpu.VMEM((model, 3 * width), bf),
            pltpu.VMEM((pairs, LANES, rows), bf),
            pltpu.VMEM((pairs, LANES, rows), bf),
            pltpu.VMEM((3, pairs, rows, LANES), bf),
            pltpu.VMEM((3, pairs, LANES, rows), bf),
            pltpu.VMEM((pairs, 2, 1, rows), f32),
            pltpu.VMEM((pairs, 2, 1, rows), f32),
            pltpu.VMEM((pairs, LANES, rows), f32),
            pltpu.VMEM((6, rows, rows), f32),
            pltpu.VMEM((pairs, LANES, rows), bf),
            pltpu.VMEM((pairs, LANES, rows), bf),
            pltpu.VMEM((pairs, 2, rows), f32),
            pltpu.VMEM((pairs, 2, rows), f32),
            pltpu.VMEM((8, LANES), f32),
            pltpu.VMEM((8, LANES), f32),
            pltpu.SemaphoreType.DMA((6,)),
            pltpu.SemaphoreType.DMA((2,)),
            pltpu.SemaphoreType.DMA((2,)),
            pltpu.SemaphoreType.DMA((pairs + 1,)),
            pltpu.SemaphoreType.DMA((pairs + 1,)),
            pltpu.SemaphoreType.DMA((pairs, 3)),
            pltpu.SemaphoreType.DMA((pairs, 3)),
            pltpu.SemaphoreType.DMA((2,)),
            pltpu.VMEM((rows, model), bf),
            pltpu.VMEM((rows, 3 * width), bf),
            pltpu.VMEM((rows, width), bf),
            pltpu.VMEM((heads, rows), f32),
            pltpu.VMEM((rows, heads), f32),
            pltpu.VMEM((rows, width), f32),
            pltpu.VMEM((64, width), f32),
            pltpu.VMEM((heads, LANES), f32),
            pltpu.VMEM((64, width), f32),
            pltpu.VMEM((64, width), f32),
            pltpu.VMEM((heads, LANES), f32),
            pltpu.VMEM((rounds, 64, width), bf),
            pltpu.VMEM((rounds, 64, width), bf),
            pltpu.VMEM((rounds, heads, LANES), f32),
            pltpu.VMEM((rounds, heads, LANES), f32),
            pltpu.SemaphoreType.DMA((rounds, 2)),
            pltpu.SemaphoreType.DMA((rounds, 2)),
        ],
        compiler_params=pltpu.CompilerParams(
            collective_id=0, has_side_effects=True, vmem_limit_bytes=60 * 2**20
        ),
    )(
        frames, norm_gain1.reshape(1, model), w_qkv1, log_decay, head_gain.reshape(1, width),
        w_out1, norm_gain2.reshape(1, model), w_qkv2, window_ids, w_out2,
    )
    parts = rows // LANES
    return pl.pallas_call(
        close_layer,
        out_shape=jax.ShapeDtypeStruct((rows, model), bf),
        in_specs=[vmem, vmem, vmem],
        out_specs=hbm,
        scratch_shapes=[
            pltpu.VMEM((rows, model), bf),
            pltpu.SemaphoreType.DMA((parts,)),
        ],
        compiler_params=pltpu.CompilerParams(vmem_limit_bytes=8 * 2**20),
    )(in_vmem(last), in_vmem(most), in_vmem(w_out2))


def solution(mesh):
    placed = (
        P(("dp", "tm"), None),
        P(),
        P(),
        P(None, ("dp", "tm")),
        P(),
        P(),
        P(),
        P(),
        P(("dp", "tm"), None),
        P(),
    )
    return jax.shard_map(
        local, mesh=mesh, in_specs=placed, out_specs=P(("dp", "tm"), None), check_vma=False
    )
```

```python
import functools

import jax
import jax.numpy as jnp
from jax import lax
from jax.experimental import pallas as pl
from jax.experimental.pallas import tpu as pltpu
from jax.sharding import PartitionSpec as P

MESH = pl.DeviceIdType.MESH
TILE = 256
WIDE = 512
FAR = -1e30
LANES = 128
SCALE2 = 1.4426950408889634


def f32dot(a, b, dims=(((1,), (0,)), ((), ()))):
    return lax.dot_general(a, b, dims, preferred_element_type=jnp.float32)


def tile_at(index, size):
    return pl.ds(pl.multiple_of(index * size, size), size)


def norm_rows(src_ref, gain_ref, dst_ref):
    step = 256

    def body(i, carry):
        rows = tile_at(i, step)
        wide = src_ref[rows, :].astype(jnp.float32)
        scale = lax.rsqrt(jnp.mean(wide * wide, axis=-1, keepdims=True) + 1e-05)
        dst_ref[rows, :] = (wide * scale * gain_ref[...]).astype(jnp.bfloat16)
        return carry

    lax.fori_loop(0, src_ref.shape[0] // step, body, 0)


def both_layers(
    n,
    x_hbm, g1_hbm, w1_hbm, ld_hbm, hg_hbm, wo_hbm, g2_hbm, w2_hbm, ids_hbm, wp_hbm,
    y_last, sum_ref,
    g1_ref, ld_ref, hg_ref, g2_ref, ids_ref, small_sem,
    wp_ref, hid_ref,
    x_ref, w1_ref, wo_ref, w2_ref, qt_ref, q_far, k_ref, v_ref,
    m_s, l_s, acc_s, s_s, o_send, o_recv, st_send, st_recv, bias_send, bias_recv,
    load_sem, kv_send, kv_recv, on_send, on_recv, far_send, far_recv, bias_sems,
    h_s, qkv_s, y_s, run_s, runt_s, lin_s, x_s, ax_s, e_s, em_s, a_s, send_b, recv_b, send_a, recv_a, send_sem, recv_sem,
):
    me = lax.axis_index("tm")
    small = [
        pltpu.make_async_copy(src, dst, small_sem.at[i])
        for i, (src, dst) in enumerate(
            [(ld_hbm, ld_ref), (g1_hbm, g1_ref), (hg_hbm, hg_ref), (g2_hbm, g2_ref), (ids_hbm, ids_ref)]
        )
    ]
    x_load = pltpu.make_async_copy(x_hbm, x_ref, load_sem.at[0])
    x_load.start()
    for load in small:
        load.start()
    rows = x_ref.shape[0]
    width = wo_ref.shape[0]
    heads = ld_ref.shape[0]
    pairs = width // LANES
    rounds = max(2, (n - 1).bit_length())
    dists = [1 << r for r in range(rounds)]

    barrier = pltpu.get_barrier_semaphore()
    for dist in dists:
        @pl.when(me + dist < n)
        def _():
            pl.semaphore_signal(barrier, inc=1, device_id={"tm": me + dist}, device_id_type=MESH)

        @pl.when(me >= dist)
        def _():
            pl.semaphore_signal(barrier, inc=1, device_id={"tm": me - dist}, device_id_type=MESH)

    loads = [
        pltpu.make_async_copy(src, dst, load_sem.at[i])
        for i, (src, dst) in enumerate(
            [
                (x_hbm, x_ref),
                (w1_hbm.at[:, width:], w1_ref.at[:, width:]),
                (w1_hbm.at[:, :width], w1_ref.at[:, :width]),
                (wo_hbm, wo_ref),
                (w2_hbm, w2_ref),
                (wp_hbm, wp_ref),
            ]
        )
    ]
    for load in loads[1:]:
        load.start()
    for load in small:
        load.wait()
    upper = (
        lax.broadcasted_iota(jnp.int32, (rows, rows), 0)
        <= lax.broadcasted_iota(jnp.int32, (rows, rows), 1)
    ).astype(jnp.float32)
    run = lax.dot_general(
        ld_ref[...], upper, (((1,), (0,)), ((), ())),
        precision=lax.Precision.HIGHEST, preferred_element_type=jnp.float32,
    )
    run_s[...] = run
    runt_s[...] = run.T
    last = run[:, rows - 1 : rows]
    headsel = lax.broadcasted_iota(jnp.int32, (heads, width), 1) // (
        width // heads
    ) == lax.broadcasted_iota(jnp.int32, (heads, width), 0)
    def by_lane(per_head):
        return jnp.sum(jnp.where(headsel, per_head[:, 0:1], 0.0), axis=0, keepdims=True)

    a_s[...] = jnp.broadcast_to(jnp.exp(last), a_s.shape)
    low = lax.broadcasted_iota(jnp.int32, (1, LANES), 1) < LANES // 2
    keeps = [jnp.where(low, 1.0 - side, float(side)).astype(jnp.bfloat16) for side in range(2)]
    half = rows // 2
    mid = run[:, half - 1 : half]
    early = lax.broadcasted_iota(jnp.int32, (heads, rows), 1) < half
    left_t = jnp.exp(jnp.where(early, mid, last) - run).T
    runt_s[half:rows, :] = runt_s[half:rows, :] - runt_s[half - 1 : half, :]
    run_s[...] = jnp.where(early, run, run - mid)
    mid_row, rest_row = by_lane(jnp.exp(mid)), by_lane(jnp.exp(last - mid))

    loads[0].wait()
    norm_rows(x_ref, g1_ref, h_s)
    loads[1].wait()

    for j in range(2):
        cols = slice(width * (j + 1), width * (j + 2))
        qkv_s[:, cols] = f32dot(h_s[...], w1_ref[:, cols]).astype(jnp.bfloat16)

    for p in range(pairs):
        cols = slice(p * LANES, (p + 1) * LANES)
        kcols = slice(width + p * LANES, width + (p + 1) * LANES)
        vcols = slice(2 * width + p * LANES, 2 * width + (p + 1) * LANES)
        decay = jnp.where(low, left_t[:, 2 * p : 2 * p + 1], left_t[:, 2 * p + 1 : 2 * p + 2])
        keyed = (qkv_s[:, kcols].astype(jnp.float32) * decay).astype(jnp.bfloat16).T
        ends = []
        for first in (0, half):
            full = f32dot(keyed[:, first : first + half], qkv_s[first : first + half, vcols])
            ends.append(jnp.where(low, full[: LANES // 2], full[LANES // 2 :]))
        em_s[:, cols] = ends[0]
        e_s[:, cols] = ends[0] * rest_row[:, cols] + ends[1]
    x_s[...] = jnp.zeros_like(x_s)
    ax_s[...] = jnp.ones_like(ax_s)

    def send(r, dist):
        @pl.when(me + dist < n)
        def _():
            send_b[r] = (e_s[...] + by_lane(a_s[...]) * x_s[...]).astype(jnp.bfloat16)
            send_a[r] = a_s[...] * ax_s[...]
            for copy in copy_of(r, dist):
                copy.start()

    def copy_of(r, dist):
        return [
            pltpu.make_async_remote_copy(
                src_ref=src.at[r], dst_ref=dst.at[r],
                send_sem=send_sem.at[r, i], recv_sem=recv_sem.at[r, i],
                device_id={"tm": me + dist}, device_id_type=MESH,
            )
            for i, (src, dst) in enumerate([(send_b, recv_b), (send_a, recv_a)])
        ]

    def receive(r, dist):
        @pl.when(me >= dist)
        def _():
            for copy in copy_of(r, dist):
                copy.wait_recv()
            x_s[...] = x_s[...] + by_lane(ax_s[...]) * recv_b[r].astype(jnp.float32)
            ax_s[...] = ax_s[...] * recv_a[r]

    peers = [me + dist < n for dist in dists] + [me >= dist for dist in dists]
    pl.semaphore_wait(barrier, sum(peer.astype(jnp.int32) for peer in peers))

    core = lax.rem(me, 2)
    even = core == 0
    odd = jnp.logical_not(even)
    helps = me + 2 < n
    helped = me >= 2
    hands_on = jnp.logical_and(odd, me + 3 < n)
    gets_prev = jnp.logical_and(even, jnp.logical_and(me >= 2, helps))

    def listing(back):
        listed = ids_ref[0, 0] == me - back
        for j in range(1, ids_ref.shape[1]):
            listed = jnp.logical_or(listed, ids_ref[0, j] == me - back)
        return jnp.where(listed, jnp.float32(0.0), jnp.float32(FAR))

    def bias_back():
        return pltpu.make_async_remote_copy(
            src_ref=bias_send, dst_ref=bias_recv,
            send_sem=bias_sems.at[0], recv_sem=bias_sems.at[1],
            device_id={"tm": me - 2}, device_id_type=MESH,
        )

    near = jnp.where(even, listing(1), listing(3))
    brow = lax.broadcasted_iota(jnp.int32, bias_send.shape, 0)
    bias_send[...] = jnp.where(brow == 0, listing(2), jnp.where(brow == 1, near, listing(3)))

    @pl.when(helped)
    def _():
        bias_back().start()

    def work_query():
        loads[2].wait()
        qkv_s[:, 0:width] = f32dot(h_s[...], w1_ref[:, 0:width]).astype(jnp.bfloat16)

    def work_pair(p):
        cols = slice(p * LANES, (p + 1) * LANES)
        kcols = slice(width + p * LANES, width + (p + 1) * LANES)
        vcols = slice(2 * width + p * LANES, 2 * width + (p + 1) * LANES)
        causal = lax.broadcasted_iota(jnp.int32, (half, half), 0) >= (
            lax.broadcasted_iota(jnp.int32, (half, half), 1)
        )
        blocks = [(first, side) for first in range(0, rows, half) for side in range(2)]
        scores = []
        for first, side in blocks:
            scores.append(
                f32dot(
                    qkv_s[first : first + half, cols] * keeps[side],
                    qkv_s[first : first + half, kcols], (((1,), (1,)), ((), ())),
                )
            )
        parts = []
        for (first, side), score in zip(blocks, scores):
            h = 2 * p + side
            diff = runt_s[first : first + half, h : h + 1] - run_s[h : h + 1, first : first + half]
            weight = jnp.exp(jnp.where(causal, jnp.minimum(diff, 0.0), FAR))
            parts.append(
                f32dot((score * weight).astype(jnp.bfloat16), qkv_s[first : first + half, vcols])
            )
        for i, first in enumerate(range(0, rows, half)):
            lin_s[first : first + half, cols] = jnp.where(low, parts[2 * i], parts[2 * i + 1])

    work = [work_query] + [functools.partial(work_pair, p) for p in range(pairs)]
    def send_after(r):
        if r < rounds:
            @pl.when(me >= (dists[r - 1] if r else 0))
            def _():
                send(r, dists[r])

        if r + 1 < rounds:
            @pl.when(jnp.logical_and(me >= (dists[r - 1] if r else 0), me < dists[r]))
            def _():
                for later in range(r + 1, rounds):
                    send(later, dists[later])

    send_after(0)
    for r, dist in enumerate(dists):
        take = 1 if r == 0 else len(work)
        for item in work[:take]:
            item()
        work = work[take:]
        receive(r, dist)
        send_after(r + 1)
    for item in work:
        item()

    side_of = [lax.broadcasted_iota(jnp.int32, (LANES, LANES), d) // 64 for d in (0, 1)]
    same_head = (side_of[0] == side_of[1]).astype(jnp.float32).astype(jnp.bfloat16)
    for p in range(pairs):
        cols = slice(p * LANES, (p + 1) * LANES)
        grow = jnp.exp(
            jnp.where(low, runt_s[:, 2 * p : 2 * p + 1], runt_s[:, 2 * p + 1 : 2 * p + 2])
        )
        scaled = (qkv_s[:, cols].astype(jnp.float32) * grow).astype(jnp.bfloat16)
        before = x_s[:, cols]
        inter = []
        for first, packed in ((0, before), (half, before * mid_row[:, cols] + em_s[:, cols])):
            state = jnp.concatenate(
                [jnp.where(low, packed, 0.0), jnp.where(low, 0.0, packed)], axis=0
            ).astype(jnp.bfloat16)
            inter.append(f32dot(scaled[first : first + half], state))
        lin = lin_s[:, cols] + jnp.concatenate(inter, axis=0)
        square = lin * lin
        high = square.astype(jnp.bfloat16)
        rest = (square - high.astype(jnp.float32)).astype(jnp.bfloat16)
        mean = (f32dot(high, same_head) + f32dot(rest, same_head)) * (1.0 / 64)
        y_s[:, cols] = (lin * lax.rsqrt(mean + 1e-06) * hg_ref[:, cols]).astype(jnp.bfloat16)

    loads[3].wait()
    for j in range(x_ref.shape[1] // WIDE):
        cols = slice(j * WIDE, (j + 1) * WIDE)
        branch = f32dot(y_s[...], wo_ref[:, cols])
        hid_ref[:, cols] = (x_ref[:, cols].astype(jnp.float32) + branch).astype(jnp.bfloat16)
    loads[4].wait()
    norm_rows(hid_ref, g2_ref, h_s)

    def query_back(p):
        return pltpu.make_async_remote_copy(
            src_ref=qt_ref.at[p], dst_ref=q_far.at[p],
            send_sem=far_send.at[p, 0], recv_sem=far_recv.at[p, 0],
            device_id={"tm": me - 2}, device_id_type=MESH,
        )

    def partial_on(p):
        return [
            pltpu.make_async_remote_copy(
                src_ref=src.at[p], dst_ref=dst.at[p],
                send_sem=far_send.at[p, i], recv_sem=far_recv.at[p, i],
                device_id={"tm": me + 2}, device_id_type=MESH,
            )
            for i, (src, dst) in [(1, (o_send, o_recv)), (2, (st_send, st_recv))]
        ]

    sib = [
        pltpu.make_async_remote_copy(
            src_ref=ref.at[0], dst_ref=ref.at[1],
            send_sem=kv_send.at[i], recv_sem=kv_recv.at[i],
            device_id={"tm": me + 1 - 2 * core}, device_id_type=MESH,
        )
        for i, ref in enumerate([k_ref, v_ref])
    ]

    def keys_on():
        return pltpu.make_async_remote_copy(
            src_ref=k_ref.at[0], dst_ref=k_ref.at[2],
            send_sem=on_send.at[pairs], recv_sem=on_recv.at[pairs],
            device_id={"tm": me + 1}, device_id_type=MESH,
        )

    def values_on(p):
        return pltpu.make_async_remote_copy(
            src_ref=v_ref.at[0, p], dst_ref=v_ref.at[2, p],
            send_sem=on_send.at[p], recv_sem=on_recv.at[p],
            device_id={"tm": me + 1}, device_id_type=MESH,
        )

    def queries():
        block = f32dot(h_s[...], w2_ref[:, 0:width]) * (SCALE2 * 64 ** (-0.5))
        for p in range(pairs):
            qt_ref[p] = block[:, p * LANES : (p + 1) * LANES].astype(jnp.bfloat16).T

            @pl.when(helped)
            def _():
                query_back(p).start()

    def keys():
        block = f32dot(h_s[...], w2_ref[:, width : 2 * width]).astype(jnp.bfloat16)
        for p in range(pairs):
            k_ref[0, p] = block[:, p * LANES : (p + 1) * LANES]

    def values():
        block = f32dot(h_s[...], w2_ref[:, 2 * width : 3 * width])
        for p in range(pairs):
            v_ref[0, p] = block[:, p * LANES : (p + 1) * LANES].astype(jnp.bfloat16).T

    @pl.when(jnp.logical_not(hands_on))
    def _():
        queries()
        keys()
        sib[0].start()
        values()
        sib[1].start()

    @pl.when(hands_on)
    def _():
        keys()
        keys_on().start()
        sib[0].start()
        values()
        for p in range(pairs):
            values_on(p).start()

        sib[1].start()
        queries()

    half_rows = LANES // 2
    blank = jnp.zeros((half_rows, rows), jnp.bfloat16)

    def pair_attend(p, query, slots, biases, put):
        def score(side):
            own = query[side * half_rows : (side + 1) * half_rows, :]
            mine = jnp.concatenate([own, blank] if side == 0 else [blank, own], axis=0)
            tops = []
            for j, slot in enumerate(slots):
                s = f32dot(k_ref[slot, p], mine)
                s_s[side * 3 + j] = s
                tops.append(jnp.max(s, axis=0, keepdims=True))
            best = functools.reduce(
                jnp.maximum, [top + bias for top, bias in zip(tops, biases)]
            )
            return best, [jnp.maximum(best - bias, top) for top, bias in zip(tops, biases)]

        def soft(side, best, refs):
            total, acc = None, None
            for j, slot in enumerate(slots):
                w = jnp.exp2(s_s[side * 3 + j] - refs[j])
                add = jnp.sum(w, axis=0, keepdims=True)
                part = f32dot(
                    v_ref[slot, p, side * half_rows : (side + 1) * half_rows, :],
                    w.astype(jnp.bfloat16),
                )
                total = add if total is None else total + add
                acc = part if acc is None else acc + part
            put(p, side, best, total, acc)

        first = score(0)
        second = score(1)
        soft(0, *first)
        soft(1, *second)

    def put_merged(p, side, best, total, acc):
        arow = slice(side * half_rows, (side + 1) * half_rows)
        m_old = m_s[p, side]
        m_new = jnp.maximum(m_old, best)
        alpha, beta = jnp.exp2(m_old - m_new), jnp.exp2(best - m_new)
        m_s[p, side] = m_new
        l_s[p, side] = l_s[p, side] * alpha + total * beta
        acc_s[p, arow, :] = acc_s[p, arow, :] * alpha + acc * beta

    def put_far(p, side, best, total, acc):
        some = total > 0.0
        inv = jnp.where(some, 1.0 / total, 0.0)
        st_send[p, side : side + 1, :] = jnp.where(some, best + jnp.log2(total), FAR)
        o_send[p, side * half_rows : (side + 1) * half_rows, :] = (acc * inv).astype(jnp.bfloat16)

    def loop_pairs(body):
        def step(p, carry):
            body(p)
            return carry

        lax.fori_loop(0, pairs, step, 0)

    own_mask = lax.broadcasted_iota(jnp.int32, (half, half), 0) <= (
        lax.broadcasted_iota(jnp.int32, (half, half), 1)
    )

    def own_attend(p):
        query = qt_ref[p]

        def score(side):
            own = query[side * half_rows : (side + 1) * half_rows, :]
            mine = jnp.concatenate([own, blank] if side == 0 else [blank, own], axis=0)
            s = f32dot(k_ref[0, p, 0:half, :], mine)
            left, right = jnp.where(own_mask, s[:, 0:half], FAR), s[:, half:rows]
            low_right = f32dot(k_ref[0, p, half:rows, :], mine[:, half:rows])
            low_right = jnp.where(own_mask, low_right, FAR)
            s_s[side, 0:half, 0:half] = left
            s_s[side, 0:half, half:rows] = right
            s_s[side, half:rows, half:rows] = low_right
            top = jnp.maximum(
                jnp.max(right, axis=0, keepdims=True), jnp.max(low_right, axis=0, keepdims=True)
            )
            return jnp.concatenate([jnp.max(left, axis=0, keepdims=True), top], axis=1)

        def soft(side, best):
            arow = slice(side * half_rows, (side + 1) * half_rows)
            w = jnp.exp2(s_s[side, 0:half, :] - best)
            late = jnp.exp2(s_s[side, half:rows, half:rows] - best[:, half:rows])
            total = jnp.sum(w, axis=0, keepdims=True)
            part = f32dot(v_ref[0, p, arow, 0:half], w.astype(jnp.bfloat16))
            more = f32dot(v_ref[0, p, arow, half:rows], late.astype(jnp.bfloat16))
            m_s[p, side] = best
            l_s[p, side, :, 0:half] = total[:, 0:half]
            l_s[p, side, :, half:rows] = total[:, half:rows] + jnp.sum(late, axis=0, keepdims=True)
            acc_s[p, arow, 0:half] = part[:, 0:half]
            acc_s[p, arow, half:rows] = part[:, half:rows] + more

        tops = [score(side) for side in range(2)]
        for side in range(2):
            soft(side, tops[side])

    loop_pairs(own_attend)
    for copy in sib:
        copy.wait_recv()

    def help_bias(j):
        return bias_recv[j : j + 1, 0:1]

    def give(p):
        for copy in partial_on(p):
            copy.start()

    def near_part(p, put):
        query_back(p).wait_recv()
        pair_attend(p, q_far[p], [0, 1], [help_bias(0), help_bias(1)], put)

    @pl.when(helps)
    def _():
        bias_back().wait_recv()

    @pl.when(gets_prev)
    def _():
        keys_on().wait_recv()
        biases = [help_bias(j) for j in range(3)]

        def body(p):
            query_back(p).wait_recv()
            values_on(p).wait_recv()
            pair_attend(p, q_far[p], [0, 1, 2], biases, put_far)
            give(p)

        loop_pairs(body)

    @pl.when(jnp.logical_and(even, jnp.logical_and(helps, jnp.logical_not(gets_prev))))
    def _():
        def body(p):
            near_part(p, put_far)
            give(p)

        loop_pairs(body)

    @pl.when(odd)
    def _():
        bias = listing(1)

        @pl.when(helps)
        def _():
            def body(p):
                near_part(p, put_far)
                give(p)

            loop_pairs(body)

        loop_pairs(lambda p: pair_attend(p, qt_ref[p], [1], [bias], put_merged))

    def most_of_output(j):
        cols = slice(j * WIDE, (j + 1) * WIDE)
        most = (pairs - 1) * LANES
        sum_ref[:, cols] = hid_ref[:, cols].astype(jnp.float32) + f32dot(
            y_s[:, 0:most], wp_ref[0:most, cols]
        )

    for p in range(pairs):
        @pl.when(helped)
        def _():
            for copy in partial_on(p):
                copy.wait_recv()
            for half in range(2):
                far = o_recv[p, half * half_rows : (half + 1) * half_rows, :]
                put_merged(
                    p, half, st_recv[p, half : half + 1, :], 1.0, far.astype(jnp.float32),
                )

        whole = jnp.concatenate(
            [
                acc_s[p, 0:half_rows, :] * (1.0 / l_s[p, 0]),
                acc_s[p, half_rows:LANES, :] * (1.0 / l_s[p, 1]),
            ],
            axis=0,
        )
        if p < pairs - 1:
            y_s[:, p * LANES : (p + 1) * LANES] = whole.T.astype(jnp.bfloat16)
        else:
            y_last[...] = whole.T.astype(jnp.bfloat16)
        if p == pairs - 2:
            loads[5].wait()
            for j in range(hid_ref.shape[1] // WIDE):
                most_of_output(j)

    def drain(copies):
        for copy in copies:
            copy.wait_send()

    for r, dist in enumerate(dists):
        @pl.when(me + dist < n)
        def _():
            for copy in copy_of(r, dist):
                copy.wait_send()

    drain(sib)

    @pl.when(hands_on)
    def _():
        drain([keys_on()] + [values_on(p) for p in range(pairs)])

    @pl.when(helped)
    def _():
        drain([bias_back()])

    for p in range(pairs):
        @pl.when(helped)
        def _():
            drain([query_back(p)])

        @pl.when(helps)
        def _():
            drain(partial_on(p))


def close_layer(y_ref, sum_ref, wp_ref, out_hbm, out_ref, sems):
    copies = []
    for i in range(out_ref.shape[0] // LANES):
        rows = slice(i * LANES, (i + 1) * LANES)
        branch = f32dot(y_ref[rows, :], wp_ref[wp_ref.shape[0] - LANES :, :])
        out_ref[rows, :] = (sum_ref[rows, :] + branch).astype(jnp.bfloat16)
        copies.append(pltpu.make_async_copy(out_ref.at[rows], out_hbm.at[rows], sems.at[i]))
        copies[-1].start()
    for copy in copies:
        copy.wait()


def in_vmem(array):
    return pltpu.with_memory_space_constraint(array, pltpu.VMEM)


def local(
    frames, norm_gain1, w_qkv1, log_decay, head_gain, w_out1, norm_gain2, w_qkv2, window_ids, w_out2
):
    n = lax.axis_size("tm")
    rows, model = frames.shape
    width = w_out1.shape[0]
    heads = log_decay.shape[0]
    rounds = max(2, (n - 1).bit_length())
    pairs = width // LANES
    vmem = pl.BlockSpec(memory_space=pltpu.VMEM)
    hbm = pl.BlockSpec(memory_space=pltpu.HBM)
    bf, f32 = jnp.bfloat16, jnp.float32
    last, most = pl.pallas_call(
        functools.partial(both_layers, n),
        out_shape=[
            pltpu.VMEM((rows, LANES), bf),
            pltpu.VMEM((rows, model), f32),
        ],
        in_specs=[hbm] * 10,
        out_specs=[vmem, vmem],
        scratch_shapes=[
            pltpu.VMEM((1, model), f32),
            pltpu.VMEM((heads, rows), f32),
            pltpu.VMEM((1, width), f32),
            pltpu.VMEM((1, model), f32),
            pltpu.SMEM(window_ids.shape, jnp.int32),
            pltpu.SemaphoreType.DMA((5,)),
            pltpu.VMEM((width, model), bf),
            pltpu.VMEM((rows, model), bf),
            pltpu.VMEM((rows, model), bf),
            pltpu.VMEM((model, 3 * width), bf),
            pltpu.VMEM((width, model), bf),
            pltpu.VMEM((model, 3 * width), bf),
            pltpu.VMEM((pairs, LANES, rows), bf),
            pltpu.VMEM((pairs, LANES, rows), bf),
            pltpu.VMEM((3, pairs, rows, LANES), bf),
            pltpu.VMEM((3, pairs, LANES, rows), bf),
            pltpu.VMEM((pairs, 2, 1, rows), f32),
            pltpu.VMEM((pairs, 2, 1, rows), f32),
            pltpu.VMEM((pairs, LANES, rows), f32),
            pltpu.VMEM((6, rows, rows), f32),
            pltpu.VMEM((pairs, LANES, rows), bf),
            pltpu.VMEM((pairs, LANES, rows), bf),
            pltpu.VMEM((pairs, 2, rows), f32),
            pltpu.VMEM((pairs, 2, rows), f32),
            pltpu.VMEM((8, LANES), f32),
            pltpu.VMEM((8, LANES), f32),
            pltpu.SemaphoreType.DMA((6,)),
            pltpu.SemaphoreType.DMA((2,)),
            pltpu.SemaphoreType.DMA((2,)),
            pltpu.SemaphoreType.DMA((pairs + 1,)),
            pltpu.SemaphoreType.DMA((pairs + 1,)),
            pltpu.SemaphoreType.DMA((pairs, 3)),
            pltpu.SemaphoreType.DMA((pairs, 3)),
            pltpu.SemaphoreType.DMA((2,)),
            pltpu.VMEM((rows, model), bf),
            pltpu.VMEM((rows, 3 * width), bf),
            pltpu.VMEM((rows, width), bf),
            pltpu.VMEM((heads, rows), f32),
            pltpu.VMEM((rows, heads), f32),
            pltpu.VMEM((rows, width), f32),
            pltpu.VMEM((64, width), f32),
            pltpu.VMEM((heads, LANES), f32),
            pltpu.VMEM((64, width), f32),
            pltpu.VMEM((64, width), f32),
            pltpu.VMEM((heads, LANES), f32),
            pltpu.VMEM((rounds, 64, width), bf),
            pltpu.VMEM((rounds, 64, width), bf),
            pltpu.VMEM((rounds, heads, LANES), f32),
            pltpu.VMEM((rounds, heads, LANES), f32),
            pltpu.SemaphoreType.DMA((rounds, 2)),
            pltpu.SemaphoreType.DMA((rounds, 2)),
        ],
        compiler_params=pltpu.CompilerParams(
            collective_id=0, has_side_effects=True, vmem_limit_bytes=60 * 2**20
        ),
    )(
        frames, norm_gain1.reshape(1, model), w_qkv1, log_decay, head_gain.reshape(1, width),
        w_out1, norm_gain2.reshape(1, model), w_qkv2, window_ids, w_out2,
    )
    parts = rows // LANES
    return pl.pallas_call(
        close_layer,
        out_shape=jax.ShapeDtypeStruct((rows, model), bf),
        in_specs=[vmem, vmem, vmem],
        out_specs=hbm,
        scratch_shapes=[
            pltpu.VMEM((rows, model), bf),
            pltpu.SemaphoreType.DMA((parts,)),
        ],
        compiler_params=pltpu.CompilerParams(vmem_limit_bytes=8 * 2**20),
    )(in_vmem(last), in_vmem(most), in_vmem(w_out2))


def solution(mesh):
    placed = (
        P(("dp", "tm"), None),
        P(),
        P(),
        P(None, ("dp", "tm")),
        P(),
        P(),
        P(),
        P(),
        P(("dp", "tm"), None),
        P(),
    )
    return jax.shard_map(
        local, mesh=mesh, in_specs=placed, out_specs=P(("dp", "tm"), None), check_vma=False
    )
```
